32 devices in a mesh: seq: 16 (over z, y, core), head: 2 (over x).
Axes of the slice: x: 2, y: 2, z: 4, core: 2. Of those that a mesh axis runs over, the one named last changes fastest.
Arguments:
- query_in: bfloat16 [6144, 512], P('seq', 'head'), may hold values from -6 to 6
- key_in: bfloat16 [6144, 512], P('seq', 'head'), may hold values from -6 to 6
- value_in: bfloat16 [6144, 512], P('seq', 'head'), may hold values from -6 to 6
- text_keys: bfloat16 [256, 512], P(None, 'head'), may hold values from -6 to 6
- text_values: bfloat16 [256, 512], P(None, 'head'), may hold values from -6 to 6
- text_mask: int32 [256], replicated, may hold values 0 or 1
- window_reach: int32 [4, 2], P('head'), may hold values from 0 to 1
- tile_map: int32 [16, 3], replicated, may hold values from 0 to 14, as said below
- out_weight: bfloat16 [512, 3072], P('head'), may hold values from -0.25 to 0.25
- gate_scale: float32 [3072], replicated, may hold values from -4 to 4
- grad_out: bfloat16 [6144, 3072], P('seq', 'head'), may hold values from -12 to 12
Outputs:
- grad_query: bfloat16 [6144, 512], P('seq', 'head')
- grad_key: bfloat16 [6144, 512], P('seq', 'head')
- grad_value: bfloat16 [6144, 512], P('seq', 'head')
- grad_text_keys: bfloat16 [256, 512], P(None, 'head')
- grad_text_values: bfloat16 [256, 512], P(None, 'head')
- grad_gate: float32 [3072], replicated
The draws below stay inside these ranges and needn't reach their ends.
Inputs may be any that keep to these rules, and one draw needn't show every extreme that they name: `tile_map`: index i of seq sits at grid row i // 8 and grid column i % 8. Its tile row is that grid row, or 1 minus it, plus an offset; its tile column is the grid column, or 7 minus it, plus an offset; the mirroring and the offsets are the same for all indices, and so is the frame coordinate. Of the two offsets, the one of the longer grid dimension (rows when they are equal) is 7, the other 0.
All inputs are finite; a program needn't handle non-finite values.
Results may differ from the reference program's by a relative error of at most 0.02035.
The reference program's roundings to bfloat16 on the way (of `queries`, `rotated_keys`, `probs`, `attn`, `grad_proj`, `grad_attn` and `grad_scores`) count: a program that leaves them out, or rounds other values in their place, can miss the bound.
Values may be sent and summed in bfloat16 or wider, within the bound.
A program may use at most 64 MiB of HBM per device.

```python
import jax
import jax.numpy as jnp
from jax import lax

D = 3072
HEAD_DIM = 128
HEADS = 4
TILE_T = 6
TILE_H = 8
TILE_W = 8
TILE = 384
COLS = 8
TXT = 256
TOKENS = 6144
N_SEQ = 16


def paired_draw(key):
    base = jax.random.fold_in(key, 7)
    first_key, second_key = jax.random.split(base, 2)
    token_total = N_SEQ * TILE_T * TILE_H * TILE_W
    feature_width = HEADS * HEAD_DIM
    queries = jnp.clip(1.5 * jax.random.normal(first_key, (token_total, feature_width), jnp.float32), -6.0, 6.0)
    keys_drawn = jnp.clip(1.5 * jax.random.normal(second_key, (token_total, feature_width), jnp.float32), -6.0, 6.0)
    return (queries, keys_drawn)


def draw_query_in(key, part):
    return paired_draw(key)[0].astype(jnp.bfloat16)


def draw_key_in(key, part):
    return paired_draw(key)[1].astype(jnp.bfloat16)


def draw_grad_out(key, part):
    base = jax.random.fold_in(key, 19)
    first_key = jax.random.fold_in(base, 0)
    token_total = N_SEQ * TILE_T * TILE_H * TILE_W
    noise = jnp.clip(jax.random.normal(first_key, (token_total, D), jnp.float32), -4.0, 4.0)
    ramp = jnp.arange(token_total, dtype=jnp.float32) / (token_total - 1)
    return (noise * (1.0 + 2.0 * ramp)[:, None]).astype(jnp.bfloat16)


def draw_tile_map(key, part):
    base = jax.random.fold_in(key, 31)
    flip_key, offset_key = jax.random.split(base)
    flips = jax.random.randint(flip_key, (2,), 0, 2)
    frame_offset = jax.random.randint(offset_key, (), 0, 5)
    device = jnp.arange(N_SEQ, dtype=jnp.int32)
    row_count = N_SEQ // COLS
    row_offset = 7 if row_count >= COLS else 0
    col_offset = 0 if row_count >= COLS else 7
    grid_row = device // COLS
    grid_col = device % COLS
    tile_row = jnp.where(flips[0] == 1, row_count - 1 - grid_row, grid_row) + row_offset
    tile_col = jnp.where(flips[1] == 1, COLS - 1 - grid_col, grid_col) + col_offset
    tile_frame = jnp.zeros_like(device) + frame_offset
    return jnp.stack([tile_frame, tile_row, tile_col], axis=1).astype(jnp.int32)


def place_ends(drawn, stream_key, smallest, top_value):
    dims = drawn.shape
    index_at = [jax.random.randint(jax.random.fold_in(stream_key, axis), (), 0, dims[axis]) for axis in range(len(dims))]
    drawn = drawn.at[tuple(index_at)].set(smallest)
    longest = dims.index(max(dims))
    index_at[longest] = (index_at[longest] + 1) % dims[longest]
    return drawn.at[tuple(index_at)].set(top_value)


def shard_levels(key, dims, shards, smallest, high):
    factor_of = 1.0
    for dim, parts in shards:
        steps = jax.random.uniform(jax.random.fold_in(jax.random.fold_in(key, 6), dim), (parts,), jnp.float32, smallest / len(shards), high / len(shards))
        factor_of = factor_of * jnp.repeat(jnp.exp(steps), dims[dim] // parts).reshape((-1,) + (1,) * (len(dims) - 1 - dim))
    return factor_of


def gaussian(key, extent, width, reach, cuts=(), kind=jnp.bfloat16):
    values = width * jax.random.normal(key, extent, jnp.float32)
    if cuts:
        values = values * shard_levels(key, extent, cuts, -0.22, 0.18)
    return jnp.clip(values, -reach, reach).astype(kind)


def setup_inputs(seed: int = 0) -> dict:
    seeds = jax.random.split(jax.random.key(seed), 12)
    query_in = draw_query_in(jax.random.fold_in(seeds[11], 71), 0)
    key_in = draw_key_in(jax.random.fold_in(seeds[11], 71), 0)
    value_in = gaussian(seeds[2], (TOKENS, HEADS * HEAD_DIM), 1.0, 6.0, ((0, 16), (1, 2)))
    text_keys = gaussian(seeds[3], (TXT, HEADS * HEAD_DIM), 1.5, 6.0, ((1, 2),))
    text_values = gaussian(seeds[4], (TXT, HEADS * HEAD_DIM), 1.0, 6.0, ((1, 2),))
    text_mask = place_ends((jax.random.randint(seeds[5], (TXT,), 0, 2) < 1).astype(jnp.int32), jax.random.fold_in(seeds[5], 1), 0, 1)
    window_reach = place_ends(jax.random.randint(seeds[6], (HEADS, 2), 0, 2), jax.random.fold_in(seeds[6], 1), 0, 1).astype(jnp.int32)
    tile_map = draw_tile_map(jax.random.fold_in(seeds[11], 71), 0)
    out_weight = gaussian(seeds[8], (HEADS * HEAD_DIM, D), (HEADS * HEAD_DIM) ** -0.5, 0.25, ((0, 2),))
    gate_scale = gaussian(seeds[9], (D,), 1.0, 4.0, (), jnp.float32)
    grad_out = draw_grad_out(jax.random.fold_in(seeds[11], 71), 0)
    return {"query_in": query_in, "key_in": key_in, "value_in": value_in, "text_keys": text_keys, "text_values": text_values, "text_mask": text_mask, "window_reach": window_reach, "tile_map": tile_map, "out_weight": out_weight, "gate_scale": gate_scale, "grad_out": grad_out}


theta_base = 256.0


def to_bf16(values):
    return lax.optimization_barrier(values.astype(jnp.bfloat16))


def sections(head_dim):
    first = head_dim // 8
    second = (head_dim - first) // 2
    return ((0, first), (first, second), (first + second, second))


def rotate(values, frame_pos, row_pos, col_pos, direction):
    pieces = []
    for (offset, length), where_pos in zip(sections(values.shape[-1]), (frame_pos, row_pos, col_pos)):
        half_len = length // 2
        freqs = theta_base ** (-2.0 * jnp.arange(half_len, dtype=jnp.float32) / length)
        angles = where_pos.astype(jnp.float32)[:, None] * freqs[None, :]
        cosine = jnp.cos(angles)[:, None, :]
        sine_part = jnp.sin(angles)[:, None, :]
        first_half = values[..., offset:offset + half_len]
        second_half = values[..., offset + half_len:offset + length]
        pieces.append(first_half * cosine - direction * second_half * sine_part)
        pieces.append(direction * first_half * sine_part + second_half * cosine)
    return jnp.concatenate(pieces, axis=-1)


def local_positions(tile_coords):
    local_index = jnp.arange(TILE_T * TILE_H * TILE_W, dtype=jnp.int32)
    plane_size = TILE_H * TILE_W
    frame_pos = tile_coords[:, 0:1] * TILE_T + (local_index // plane_size)[None, :]
    row_pos = tile_coords[:, 1:2] * TILE_H + ((local_index // TILE_W) % TILE_H)[None, :]
    col_pos = tile_coords[:, 2:3] * TILE_W + (local_index % TILE_W)[None, :]
    return frame_pos.reshape(-1), row_pos.reshape(-1), col_pos.reshape(-1)


def reference(query_in, key_in, value_in, text_keys, text_values, text_mask, window_reach, tile_map, out_weight, gate_scale, grad_out):
    score_scale = HEAD_DIM ** -0.5
    head_shape = (TOKENS, HEADS, HEAD_DIM)
    tile_shape = (N_SEQ, TILE, HEADS, HEAD_DIM)
    frame_pos, row_pos, col_pos = local_positions(tile_map)
    queries = to_bf16(rotate(query_in.astype(jnp.float32).reshape(head_shape), frame_pos, row_pos, col_pos, 1.0))
    rotated_keys = to_bf16(rotate(key_in.astype(jnp.float32).reshape(head_shape), frame_pos, row_pos, col_pos, 1.0))
    queries_t = queries.reshape(tile_shape)
    keys_t = rotated_keys.reshape(tile_shape)
    values_t = value_in.reshape(tile_shape)

    row_count = N_SEQ // COLS
    row_rel = tile_map[:, 1] - jnp.min(tile_map[:, 1])
    col_rel = tile_map[:, 2] - jnp.min(tile_map[:, 2])
    lookup = jnp.zeros((row_count, COLS), jnp.int32).at[row_rel, col_rel].set(jnp.arange(N_SEQ, dtype=jnp.int32))
    row_steps = jnp.array([-1, -1, -1, 0, 0, 0, 1, 1, 1], jnp.int32)
    col_steps = jnp.array([-1, 0, 1, -1, 0, 1, -1, 0, 1], jnp.int32)
    near_row = row_rel[:, None] + row_steps[None, :]
    near_col = col_rel[:, None] + col_steps[None, :]
    usable = (near_row >= 0) & (near_row < row_count) & (near_col >= 0) & (near_col < COLS)
    near = lookup[jnp.clip(near_row, 0, row_count - 1), jnp.clip(near_col, 0, COLS - 1)]
    allowed = usable[:, :, None] & (jnp.abs(row_steps)[None, :, None] <= window_reach[None, None, :, 0]) & (jnp.abs(col_steps)[None, :, None] <= window_reach[None, None, :, 1])

    text_open = text_mask == 1
    text_keys_f = text_keys.astype(jnp.float32).reshape(TXT, HEADS, HEAD_DIM)
    text_values_f = text_values.astype(jnp.float32).reshape(TXT, HEADS, HEAD_DIM)
    video_keys = 9 * TILE

    def key_set(index):
        near_keys = keys_t[near[index]].astype(jnp.float32).reshape(video_keys, HEADS, HEAD_DIM)
        near_values = values_t[near[index]].astype(jnp.float32).reshape(video_keys, HEADS, HEAD_DIM)
        all_keys = jnp.concatenate([near_keys, text_keys_f], axis=0)
        all_values = jnp.concatenate([near_values, text_values_f], axis=0)
        block_mask = jnp.repeat(allowed[index].T, TILE, axis=1)
        full_mask = jnp.concatenate([block_mask, jnp.broadcast_to(text_open[None, :], (HEADS, TXT))], axis=1)
        return all_keys, all_values, full_mask

    def forward_tile(index):
        all_keys, all_values, full_mask = key_set(index)
        query_f = queries_t[index].astype(jnp.float32)
        scores = jnp.einsum("qhd,khd->hqk", query_f, all_keys) * score_scale
        scores = jnp.where(full_mask[:, None, :], scores, -jnp.inf)
        peak = jnp.max(scores, axis=-1)
        log_norm = peak + jnp.log(jnp.sum(jnp.exp(scores - peak[..., None]), axis=-1))
        weights = jnp.where(full_mask[:, None, :], jnp.exp(scores - log_norm[..., None]), 0.0)
        probs = to_bf16(weights).astype(jnp.float32)
        attn = to_bf16(jnp.einsum("hqk,khd->qhd", probs, all_values))
        return log_norm, attn

    log_norms, attn = lax.map(forward_tile, jnp.arange(N_SEQ, dtype=jnp.int32))
    attn_flat = attn.reshape(TOKENS, HEADS * HEAD_DIM)
    grad_proj = to_bf16(grad_out.astype(jnp.float32) * gate_scale[None, :])
    grad_attn = to_bf16(jnp.dot(grad_proj, out_weight.T, preferred_element_type=jnp.float32))
    projected = jnp.dot(attn_flat, out_weight, preferred_element_type=jnp.float32)
    grad_gate = jnp.sum(grad_out.astype(jnp.float32) * projected, axis=0)
    grad_t = grad_attn.reshape(tile_shape)
    deltas = jnp.einsum("nqhd,nqhd->nhq", grad_t.astype(jnp.float32), attn.astype(jnp.float32))

    def query_tile(index):
        all_keys, all_values, full_mask = key_set(index)
        query_f = queries_t[index].astype(jnp.float32)
        grad_f = grad_t[index].astype(jnp.float32)
        scores = jnp.einsum("qhd,khd->hqk", query_f, all_keys) * score_scale
        weights = jnp.where(full_mask[:, None, :], jnp.exp(scores - log_norms[index][..., None]), 0.0)
        grad_weights = jnp.einsum("qhd,khd->hqk", grad_f, all_values)
        grad_scores = to_bf16(weights * (grad_weights - deltas[index][..., None])).astype(jnp.float32)
        grad_q = jnp.einsum("hqk,khd->qhd", grad_scores, all_keys) * score_scale
        text_key_part = jnp.einsum("hqk,qhd->khd", grad_scores[:, :, video_keys:], query_f) * score_scale
        text_probs = to_bf16(weights[:, :, video_keys:]).astype(jnp.float32)
        text_value_part = jnp.einsum("hqk,qhd->khd", text_probs, grad_f)
        return grad_q, text_key_part, text_value_part

    grad_qs, text_key_parts, text_value_parts = lax.map(query_tile, jnp.arange(N_SEQ, dtype=jnp.int32))

    def key_tile(index):
        near_index = near[index]
        query_f = queries_t[near_index].astype(jnp.float32).reshape(video_keys, HEADS, HEAD_DIM)
        grad_f = grad_t[near_index].astype(jnp.float32).reshape(video_keys, HEADS, HEAD_DIM)
        norms_near = log_norms[near_index].transpose(1, 0, 2).reshape(HEADS, video_keys)
        deltas_near = deltas[near_index].transpose(1, 0, 2).reshape(HEADS, video_keys)
        block_mask = jnp.repeat(allowed[index].T, TILE, axis=1)
        key_f = keys_t[index].astype(jnp.float32)
        value_f = values_t[index].astype(jnp.float32)
        scores = jnp.einsum("qhd,khd->hqk", query_f, key_f) * score_scale
        weights = jnp.where(block_mask[:, :, None], jnp.exp(scores - norms_near[:, :, None]), 0.0)
        grad_weights = jnp.einsum("qhd,khd->hqk", grad_f, value_f)
        grad_scores = to_bf16(weights * (grad_weights - deltas_near[:, :, None])).astype(jnp.float32)
        key_part = jnp.einsum("hqk,qhd->khd", grad_scores, query_f) * score_scale
        value_part = jnp.einsum("hqk,qhd->khd", to_bf16(weights).astype(jnp.float32), grad_f)
        return key_part, value_part

    key_parts, value_parts = lax.map(key_tile, jnp.arange(N_SEQ, dtype=jnp.int32))
    flat_width = HEADS * HEAD_DIM
    grad_query = rotate(grad_qs.reshape(head_shape), frame_pos, row_pos, col_pos, -1.0).astype(jnp.bfloat16).reshape(TOKENS, flat_width)
    grad_key = rotate(key_parts.reshape(head_shape), frame_pos, row_pos, col_pos, -1.0).astype(jnp.bfloat16).reshape(TOKENS, flat_width)
    grad_value = value_parts.reshape(TOKENS, flat_width).astype(jnp.bfloat16)
    grad_text_keys = jnp.sum(text_key_parts, axis=0).reshape(TXT, flat_width).astype(jnp.bfloat16)
    grad_text_values = jnp.sum(text_value_parts, axis=0).reshape(TXT, flat_width).astype(jnp.bfloat16)
    return grad_query, grad_key, grad_value, grad_text_keys, grad_text_values, grad_gate
```

```python
import functools

import jax
import jax.numpy as jnp
import numpy as np
from jax import lax
from jax.experimental import pallas as pl
from jax.experimental.pallas import tpu as pltpu
from jax.sharding import PartitionSpec as P

HEAD_DIM = 128
TILE_T = 6
TILE_H = 8
TILE_W = 8
COLS = 8
THETA = 256.0
NEG = -1e30
F32 = jnp.float32
BF16 = jnp.bfloat16


def lane_tables():
    first = HEAD_DIM // 8
    second = (HEAD_DIM - first) // 2
    freqs = np.zeros((HEAD_DIM,), np.float32)
    section = np.zeros((HEAD_DIM,), np.float32)
    sign = np.zeros((HEAD_DIM,), np.float32)
    offset = 0
    for number, length in enumerate((first, second, second)):
        half = length // 2
        f = (THETA ** (-2.0 * np.arange(half) / length)).astype(np.float32)
        freqs[offset : offset + half] = f
        freqs[offset + half : offset + length] = f
        section[offset : offset + length] = number
        sign[offset : offset + half] = -1.0
        sign[offset + half : offset + length] = 1.0
        offset += length
    return np.stack([freqs, section, sign] + [np.zeros_like(freqs)] * 5)


def partner(x):
    first = HEAD_DIM // 8
    second = (HEAD_DIM - first) // 2
    lane = lax.broadcasted_iota(jnp.int32, x.shape, 1)
    a = first // 2
    b = second // 2
    up_a = pltpu.roll(x, HEAD_DIM - a, 1)
    down_a = pltpu.roll(x, a, 1)
    up_b = pltpu.roll(x, HEAD_DIM - b, 1)
    down_b = pltpu.roll(x, b, 1)
    in_a = jnp.where(lane < a, up_a, down_a)
    is_first = (lane < first + b) | ((lane >= first + second) & (lane < first + second + b))
    in_b = jnp.where(is_first, up_b, down_b)
    return jnp.where(lane < first, in_a, in_b)


def prep_kernel(heads, tile_ref, lanes_ref, q_ref, k_ref, v_ref, qr_ref, kv_ref, cos_ref, sin_ref):
    device = lax.axis_index("seq")
    freqs = lanes_ref[0:1, :]
    section = lanes_ref[1:2, :]
    sign = lanes_ref[2:3, :]

    def table(count, base):
        step = lax.broadcasted_iota(jnp.int32, (8, HEAD_DIM), 0)
        pos = (base * count + step).astype(F32)
        angle = pos * freqs
        return jnp.cos(angle), jnp.sin(angle) * sign

    cf, sf = table(TILE_T, tile_ref[device, 0])
    cr, sr = table(TILE_H, tile_ref[device, 1])
    cc, sc = table(TILE_W, tile_ref[device, 2])
    for t in range(TILE_T):
        for r in range(TILE_H):
            at = pl.ds((t * TILE_H + r) * TILE_W, TILE_W)
            for out, f, w, c in ((cos_ref, cf, cr, cc), (sin_ref, sf, sr, sc)):
                low = jnp.where(section == 0.0, f[t : t + 1, :], w[r : r + 1, :])
                full = jnp.broadcast_to(section, c.shape)
                out[at, :] = jnp.where(full < 2.0, jnp.broadcast_to(low, c.shape), c)
    cosine = cos_ref[...]
    sine = sin_ref[...]
    for h in range(heads):
        cols = slice(h * HEAD_DIM, (h + 1) * HEAD_DIM)
        x = q_ref[:, cols].astype(F32)
        qr_ref[:, cols] = (x * cosine + partner(x) * sine).astype(BF16)
        x = k_ref[:, cols].astype(F32)
        kv_ref[0, :, cols] = (x * cosine + partner(x) * sine).astype(BF16)
    kv_ref[1] = v_ref[...]


def attend_kernel(
    deltas,
    row_count,
    reach_ref,
    mask_ref,
    q_ref,
    g_ref,
    kv_ref,
    tk_ref,
    tv_ref,
    cos_ref,
    sin_ref,
    attn_ref,
    dq_ref,
    part_ref,
    dtk_ref,
    dtv_ref,
    s_ref,
    m_ref,
    l_ref,
    o_ref,
    dqa_ref,
):
    head = pl.program_id(0)
    device = lax.axis_index("seq")
    row = device // COLS
    col = device % COLS
    tile = q_ref.shape[0]
    text = tk_ref.shape[0]
    scale = HEAD_DIM ** (-0.5)
    reach_r = reach_ref[head, 0]
    reach_c = reach_ref[head, 1]
    q = q_ref[...]
    g = g_ref[...]
    blocks = []
    for number, (dr, dc) in enumerate(deltas):
        ok = (abs(dr) <= reach_r) & (abs(dc) <= reach_c)
        ok = ok & (col + dc >= 0) & (col + dc < COLS)
        if row_count > 2:
            ok = ok & (row + dr >= 0) & (row + dr < row_count)
        blocks.append((number, ok))
    nb = len(deltas)
    text_at = slice(nb * tile, nb * tile + text)

    def nt(a, b):
        return lax.dot_general(a, b, (((1,), (1,)), ((), ())), preferred_element_type=F32)

    def tn(a, b):
        return lax.dot_general(a, b, (((0,), (0,)), ((), ())), preferred_element_type=F32)

    def nn(a, b):
        return lax.dot_general(a, b, (((1,), (0,)), ((), ())), preferred_element_type=F32)

    s = nt(tk_ref[...], q) * scale
    s = jnp.where(mask_ref[...] == 1, s, NEG)
    s_ref[text_at, :] = s
    m_ref[...] = jnp.max(s, axis=0, keepdims=True)
    for number, ok in blocks:
        at = slice(number * tile, (number + 1) * tile)

        @pl.when(ok)
        def _():
            s = nt(kv_ref[number, 0], q) * scale
            s_ref[at, :] = s
            m_ref[...] = jnp.maximum(m_ref[...], jnp.max(s, axis=0, keepdims=True))

    e = jnp.exp(s_ref[text_at, :] - m_ref[...])
    s_ref[text_at, :] = e
    l_ref[...] = jnp.sum(e, axis=0, keepdims=True)
    for number, ok in blocks:
        at = slice(number * tile, (number + 1) * tile)

        @pl.when(ok)
        def _():
            e = jnp.exp(s_ref[at, :] - m_ref[...])
            s_ref[at, :] = e
            l_ref[...] += jnp.sum(e, axis=0, keepdims=True)

    inv = 1.0 / l_ref[...]
    l_ref[...] = inv
    p = (s_ref[text_at, :] * inv).astype(BF16)
    o_ref[...] = tn(tv_ref[...], p)
    dtv_ref[...] = nn(p, g)
    for number, ok in blocks:
        at = slice(number * tile, (number + 1) * tile)

        @pl.when(ok)
        def _():
            p = (s_ref[at, :] * l_ref[...]).astype(BF16)
            o_ref[...] += tn(kv_ref[number, 1], p)
            part_ref[number, 1] = nn(p, g).astype(BF16)

        @pl.when(jnp.logical_not(ok))
        def _():
            part_ref[number] = jnp.zeros(part_ref.shape[1:], BF16)

    attn = o_ref[...].T.astype(BF16)
    attn_ref[...] = attn
    delta_rows = g.astype(F32) * attn.astype(F32)
    delta = jnp.sum(delta_rows.T, axis=0, keepdims=True)
    m_ref[...] = delta
    ds = (s_ref[text_at, :] * l_ref[...] * (nt(tv_ref[...], g) - delta)).astype(BF16)
    dqa_ref[...] = tn(tk_ref[...], ds)
    dtk_ref[...] = nn(ds, q) * scale
    for number, ok in blocks:
        at = slice(number * tile, (number + 1) * tile)

        @pl.when(ok)
        def _():
            dp = nt(kv_ref[number, 1], g)
            ds = (s_ref[at, :] * l_ref[...] * (dp - m_ref[...])).astype(BF16)
            dqa_ref[...] += tn(kv_ref[number, 0], ds)
            part_ref[number, 0] = (nn(ds, q) * scale).astype(BF16)

    dq = dqa_ref[...].T * scale
    dq_ref[...] = (dq * cos_ref[...] - partner(dq) * sin_ref[...]).astype(BF16)


def post_kernel(heads, count, *refs):
    parts = refs[:count]
    cos_ref, sin_ref, dk_ref, dv_ref = refs[count:]
    cosine = cos_ref[...]
    sine = sin_ref[...]
    for h in range(heads):
        cols = slice(h * HEAD_DIM, (h + 1) * HEAD_DIM)
        dk = parts[0][0, :, cols].astype(F32)
        dv = parts[0][1, :, cols].astype(F32)
        for part in parts[1:]:
            dk = dk + part[0, :, cols].astype(F32)
            dv = dv + part[1, :, cols].astype(F32)
        dk_ref[:, cols] = (dk * cosine - partner(dk) * sine).astype(BF16)
        dv_ref[:, cols] = dv.astype(BF16)


def shift(array, dr, dc, row_count):
    pairs = []
    for r in range(row_count):
        for c in range(COLS):
            to_r, to_c = r + dr, c + dc
            if row_count == 2:
                to_r = to_r % 2
            if 0 <= to_r < row_count and 0 <= to_c < COLS:
                pairs.append((r * COLS + c, to_r * COLS + to_c))
    return lax.ppermute(array, "seq", pairs)


def on_device(
    query_in,
    key_in,
    value_in,
    text_keys,
    text_values,
    text_mask,
    window_reach,
    tile_map,
    out_weight,
    gate_scale,
    grad_out,
):
    tile, width = query_in.shape
    heads = width // HEAD_DIM
    text = text_keys.shape[0]
    seq_count = lax.axis_size("seq")
    head_count = lax.axis_size("head")
    row_count = seq_count // COLS
    device = lax.axis_index("seq")
    mine = lax.axis_index("head")
    my_cols = grad_out.shape[1]
    vmem = pl.BlockSpec(memory_space=pltpu.VMEM)
    smem = pl.BlockSpec(memory_space=pltpu.SMEM)

    q_rot, kv, cosine, sine = pl.pallas_call(
        functools.partial(prep_kernel, heads),
        out_shape=(
            jax.ShapeDtypeStruct((tile, width), BF16),
            jax.ShapeDtypeStruct((2, tile, width), BF16),
            jax.ShapeDtypeStruct((tile, HEAD_DIM), F32),
            jax.ShapeDtypeStruct((tile, HEAD_DIM), F32),
        ),
        in_specs=[smem, vmem, vmem, vmem, vmem],
        out_specs=(vmem, vmem, vmem, vmem),
    )(tile_map, jnp.asarray(lane_tables()), query_in, key_in, value_in)

    row_deltas = (0,) if row_count == 1 else (0, 1) if row_count == 2 else (0, -1, 1)
    deltas = [(dr, dc) for dr in row_deltas for dc in (0, -1, 1)]
    by_row = {dr: kv if dr == 0 else shift(kv, -dr, 0, row_count) for dr in row_deltas}
    fetched = [by_row[dr] if dc == 0 else shift(by_row[dr], 0, -dc, row_count) for dr, dc in deltas]

    core = device % 2
    half = width // 2
    rows = [None] * head_count
    own_cols = lax.dynamic_slice_in_dim(out_weight, mine * my_cols, my_cols, 1)
    pieces = [own_cols]
    swap = [(i, i ^ 1) for i in range(seq_count)]
    for step in range(1, head_count):
        to = (mine + step) % head_count
        block = lax.dynamic_slice(out_weight, (core * half, to * my_cols), (half, my_cols))
        ring = [(i, (i + step) % head_count) for i in range(head_count)]
        got = lax.ppermute(block, "head", ring)
        other = lax.ppermute(got, "seq", swap)
        pieces.append(
            jnp.concatenate(
                [jnp.where(core == 0, got, other), jnp.where(core == 0, other, got)], axis=0
            )
        )
    grad_f = grad_out.astype(F32)
    gate_cols = lax.dynamic_slice_in_dim(gate_scale, mine * my_cols, my_cols, 0)
    grad_proj = (grad_f * gate_cols[None, :]).astype(BF16)
    total = lax.dot_general(grad_proj, pieces[0], (((1,), (1,)), ((), ())), preferred_element_type=F32)
    for step in range(1, head_count):
        part = lax.dot_general(
            grad_proj, pieces[step], (((1,), (1,)), ((), ())), preferred_element_type=F32
        ).astype(BF16)
        back = [(i, (i - step) % head_count) for i in range(head_count)]
        total = total + lax.ppermute(part, "head", back).astype(F32)
    grad_attn = total.astype(BF16)

    nb = len(deltas)
    blocks = jnp.stack(fetched)
    head_spec = pl.BlockSpec((tile, HEAD_DIM), lambda h: (0, h))
    text_spec = pl.BlockSpec((text, HEAD_DIM), lambda h: (0, h))
    block_spec = pl.BlockSpec((nb, 2, tile, HEAD_DIM), lambda h: (0, 0, 0, h))
    table_spec = pl.BlockSpec((tile, HEAD_DIM), lambda h: (0, 0))
    attn, grad_query, partials, text_key_grad, text_value_grad = pl.pallas_call(
        functools.partial(attend_kernel, deltas, row_count),
        grid=(heads,),
        out_shape=(
            jax.ShapeDtypeStruct((tile, width), BF16),
            jax.ShapeDtypeStruct((tile, width), BF16),
            jax.ShapeDtypeStruct((nb, 2, tile, width), BF16),
            jax.ShapeDtypeStruct((text, width), F32),
            jax.ShapeDtypeStruct((text, width), F32),
        ),
        in_specs=[
            smem,
            pl.BlockSpec((text, 1), lambda h: (0, 0)),
            head_spec,
            head_spec,
            block_spec,
            text_spec,
            text_spec,
            table_spec,
            table_spec,
        ],
        out_specs=(head_spec, head_spec, block_spec, text_spec, text_spec),
        scratch_shapes=[
            pltpu.VMEM((nb * tile + text, tile), F32),
            pltpu.VMEM((1, tile), F32),
            pltpu.VMEM((1, tile), F32),
            pltpu.VMEM((HEAD_DIM, tile), F32),
            pltpu.VMEM((HEAD_DIM, tile), F32),
        ],
        compiler_params=pltpu.CompilerParams(vmem_limit_bytes=48 * 1024 * 1024),
    )(
        window_reach,
        text_mask[:, None],
        q_rot,
        grad_attn,
        blocks,
        text_keys,
        text_values,
        cosine,
        sine,
    )

    projected = jnp.dot(attn, pieces[0], preferred_element_type=F32)
    for step in range(1, head_count):
        ring = [(i, (i + step) % head_count) for i in range(head_count)]
        projected = projected + jnp.dot(
            lax.ppermute(attn, "head", ring), pieces[step], preferred_element_type=F32
        )
    terms = jnp.sum(grad_f * projected, axis=0)

    arrived = []
    for number_row, dr in enumerate(row_deltas):
        own = [partials[number_row * 3]]
        for offset, dc in ((1, -1), (2, 1)):
            own.append(shift(partials[number_row * 3 + offset], 0, dc, row_count))
        if dr == 0:
            arrived.extend(own)
        else:
            summed = (own[0].astype(F32) + own[1].astype(F32) + own[2].astype(F32)).astype(BF16)
            arrived.append(shift(summed, dr, 0, row_count))
    grad_key, grad_value = pl.pallas_call(
        functools.partial(post_kernel, heads, len(arrived)),
        out_shape=(
            jax.ShapeDtypeStruct((tile, width), BF16),
            jax.ShapeDtypeStruct((tile, width), BF16),
        ),
        in_specs=[vmem] * (len(arrived) + 2),
        out_specs=(vmem, vmem),
    )(*arrived, cosine, sine)

    text_key_sum, text_value_sum, gate_part = lax.psum(
        (text_key_grad, text_value_grad, terms), "seq"
    )
    grad_gate = lax.all_gather(gate_part, "head", axis=0, tiled=True)
    return (
        grad_query,
        grad_key,
        grad_value,
        text_key_sum.astype(BF16),
        text_value_sum.astype(BF16),
        grad_gate,
    )


def solution(mesh):
    placed = (
        P("seq", "head"),
        P("seq", "head"),
        P("seq", "head"),
        P(None, "head"),
        P(None, "head"),
        P(),
        P("head", None),
        P(),
        P("head", None),
        P(),
        P("seq", "head"),
    )
    return jax.shard_map(
        on_device,
        mesh=mesh,
        in_specs=placed,
        out_specs=(
            P("seq", "head"),
            P("seq", "head"),
            P("seq", "head"),
            P(None, "head"),
            P(None, "head"),
            P(),
        ),
        check_vma=False,
    )
```

```python
import functools

import jax
import jax.numpy as jnp
import numpy as np
from jax import lax
from jax.experimental import pallas as pl
from jax.experimental.pallas import tpu as pltpu
from jax.sharding import PartitionSpec as P

HEAD_DIM = 128
TILE_T = 6
TILE_H = 8
TILE_W = 8
COLS = 8
THETA = 256.0
NEG = -1e30
F32 = jnp.float32
BF16 = jnp.bfloat16
MESH = pl.DeviceIdType.MESH


def lane_tables():
    first = HEAD_DIM // 8
    second = (HEAD_DIM - first) // 2
    freqs = np.zeros((HEAD_DIM,), np.float32)
    section = np.zeros((HEAD_DIM,), np.float32)
    sign = np.zeros((HEAD_DIM,), np.float32)
    offset = 0
    for number, length in enumerate((first, second, second)):
        half = length // 2
        f = (THETA ** (-2.0 * np.arange(half) / length)).astype(np.float32)
        freqs[offset : offset + half] = f
        freqs[offset + half : offset + length] = f
        section[offset : offset + length] = number
        sign[offset : offset + half] = -1.0
        sign[offset + half : offset + length] = 1.0
        offset += length
    return np.stack([freqs, section, sign] + [np.zeros_like(freqs)] * 5)


def partner(x):
    first = HEAD_DIM // 8
    second = (HEAD_DIM - first) // 2
    lane = lax.broadcasted_iota(jnp.int32, x.shape, 1)
    a = first // 2
    b = second // 2
    up_a = pltpu.roll(x, HEAD_DIM - a, 1)
    down_a = pltpu.roll(x, a, 1)
    up_b = pltpu.roll(x, HEAD_DIM - b, 1)
    down_b = pltpu.roll(x, b, 1)
    in_a = jnp.where(lane < a, up_a, down_a)
    is_first = (lane < first + b) | ((lane >= first + second) & (lane < first + second + b))
    in_b = jnp.where(is_first, up_b, down_b)
    return jnp.where(lane < first, in_a, in_b)


def prep_kernel(heads, tile_ref, lanes_ref, q_ref, k_ref, v_ref, qr_ref, kv_ref, cos_ref, sin_ref):
    device = lax.axis_index("seq")
    freqs = lanes_ref[0:1, :]
    section = lanes_ref[1:2, :]
    sign = lanes_ref[2:3, :]

    def table(count, base):
        step = lax.broadcasted_iota(jnp.int32, (8, HEAD_DIM), 0)
        pos = (base * count + step).astype(F32)
        angle = pos * freqs
        return jnp.cos(angle), jnp.sin(angle) * sign

    cf, sf = table(TILE_T, tile_ref[device, 0])
    cr, sr = table(TILE_H, tile_ref[device, 1])
    cc, sc = table(TILE_W, tile_ref[device, 2])
    for t in range(TILE_T):
        for r in range(TILE_H):
            at = pl.ds((t * TILE_H + r) * TILE_W, TILE_W)
            for out, f, w, c in ((cos_ref, cf, cr, cc), (sin_ref, sf, sr, sc)):
                low = jnp.where(section == 0.0, f[t : t + 1, :], w[r : r + 1, :])
                full = jnp.broadcast_to(section, c.shape)
                out[at, :] = jnp.where(full < 2.0, jnp.broadcast_to(low, c.shape), c)
    cosine = cos_ref[...]
    sine = sin_ref[...]
    for h in range(heads):
        cols = slice(h * HEAD_DIM, (h + 1) * HEAD_DIM)
        x = q_ref[:, cols].astype(F32)
        qr_ref[:, cols] = (x * cosine + partner(x) * sine).astype(BF16)
        x = k_ref[:, cols].astype(F32)
        kv_ref[0, :, cols] = (x * cosine + partner(x) * sine).astype(BF16)
    kv_ref[1] = v_ref[...]


def attend_kernel(
    deltas,
    row_count,
    reach_ref,
    mask_ref,
    q_ref,
    g_ref,
    kv_ref,
    tk_ref,
    tv_ref,
    cos_ref,
    sin_ref,
    attn_ref,
    dq_ref,
    part_ref,
    dtk_ref,
    dtv_ref,
    s_ref,
    m_ref,
    l_ref,
    o_ref,
    dqa_ref,
):
    head = pl.program_id(0)
    device = lax.axis_index("seq")
    row = device // COLS
    col = device % COLS
    tile = q_ref.shape[0]
    text = tk_ref.shape[0]
    scale = HEAD_DIM ** (-0.5)
    reach_r = reach_ref[head, 0]
    reach_c = reach_ref[head, 1]
    q = q_ref[...]
    g = g_ref[...]
    blocks = []
    for number, (dr, dc) in enumerate(deltas):
        ok = (abs(dr) <= reach_r) & (abs(dc) <= reach_c)
        ok = ok & (col + dc >= 0) & (col + dc < COLS)
        if row_count > 2:
            ok = ok & (row + dr >= 0) & (row + dr < row_count)
        blocks.append((number, ok))
    nb = len(deltas)
    text_at = slice(nb * tile, nb * tile + text)

    def nt(a, b):
        return lax.dot_general(a, b, (((1,), (1,)), ((), ())), preferred_element_type=F32)

    def tn(a, b):
        return lax.dot_general(a, b, (((0,), (0,)), ((), ())), preferred_element_type=F32)

    def nn(a, b):
        return lax.dot_general(a, b, (((1,), (0,)), ((), ())), preferred_element_type=F32)

    s = nt(tk_ref[...], q) * scale
    s = jnp.where(mask_ref[...] == 1, s, NEG)
    s_ref[text_at, :] = s
    m_ref[...] = jnp.max(s, axis=0, keepdims=True)
    for number, ok in blocks:
        at = slice(number * tile, (number + 1) * tile)

        @pl.when(ok)
        def _():
            s = nt(kv_ref[number, 0], q) * scale
            s_ref[at, :] = s
            m_ref[...] = jnp.maximum(m_ref[...], jnp.max(s, axis=0, keepdims=True))

    e = jnp.exp(s_ref[text_at, :] - m_ref[...])
    s_ref[text_at, :] = e
    l_ref[...] = jnp.sum(e, axis=0, keepdims=True)
    for number, ok in blocks:
        at = slice(number * tile, (number + 1) * tile)

        @pl.when(ok)
        def _():
            e = jnp.exp(s_ref[at, :] - m_ref[...])
            s_ref[at, :] = e
            l_ref[...] += jnp.sum(e, axis=0, keepdims=True)

    inv = 1.0 / l_ref[...]
    l_ref[...] = inv
    p = (s_ref[text_at, :] * inv).astype(BF16)
    o_ref[...] = tn(tv_ref[...], p)
    dtv_ref[...] = nn(p, g)
    for number, ok in blocks:
        at = slice(number * tile, (number + 1) * tile)

        @pl.when(ok)
        def _():
            p = (s_ref[at, :] * l_ref[...]).astype(BF16)
            o_ref[...] += tn(kv_ref[number, 1], p)
            part_ref[0, number, 1] = nn(p, g).astype(BF16)

        @pl.when(jnp.logical_not(ok))
        def _():
            part_ref[0, number] = jnp.zeros(part_ref.shape[2:], BF16)

    attn = o_ref[...].T.astype(BF16)
    attn_ref[...] = attn
    delta_rows = g.astype(F32) * attn.astype(F32)
    delta = jnp.sum(delta_rows.T, axis=0, keepdims=True)
    m_ref[...] = delta
    ds = (s_ref[text_at, :] * l_ref[...] * (nt(tv_ref[...], g) - delta)).astype(BF16)
    dqa_ref[...] = tn(tk_ref[...], ds)
    dtk_ref[...] = nn(ds, q) * scale
    for number, ok in blocks:
        at = slice(number * tile, (number + 1) * tile)

        @pl.when(ok)
        def _():
            dp = nt(kv_ref[number, 1], g)
            ds = (s_ref[at, :] * l_ref[...] * (dp - m_ref[...])).astype(BF16)
            dqa_ref[...] += tn(kv_ref[number, 0], ds)
            part_ref[0, number, 0] = (nn(ds, q) * scale).astype(BF16)

    dq = dqa_ref[...].T * scale
    dq_ref[...] = (dq * cos_ref[...] - partner(dq) * sin_ref[...]).astype(BF16)


def neighbour(row, col, dr, dc, row_count):
    to_r, to_c = row + dr, col + dc
    ok = (to_c >= 0) & (to_c < COLS)
    if row_count == 2:
        to_r = (to_r + 2) % 2
    else:
        ok = ok & (to_r >= 0) & (to_r < row_count)
    return to_r * COLS + to_c, ok


def greet(axis_devices):
    barrier = pltpu.get_barrier_semaphore()
    for target, ok in axis_devices:
        if ok is None:
            pl.semaphore_signal(barrier, inc=1, device_id=target, device_id_type=MESH)
        else:

            @pl.when(ok)
            def _():
                pl.semaphore_signal(barrier, inc=1, device_id=target, device_id_type=MESH)

    count = 0
    for _, ok in axis_devices:
        count = count + (1 if ok is None else ok.astype(jnp.int32))
    pl.semaphore_wait(barrier, count)


def guarded(ok, act):
    if ok is None:
        act()
    else:
        pl.when(ok)(act)


def tail_kernel(
    row_deltas,
    row_count,
    seq_count,
    head_count,
    attn_ref,
    part_ref,
    dtk_ref,
    dtv_ref,
    w_ref,
    grad_ref,
    cos_ref,
    sin_ref,
    dk_ref,
    dv_ref,
    tk_ref,
    tv_ref,
    gate_ref,
    attn_in,
    col_in,
    row_out,
    row_in,
    acc,
    text_out,
    text_in,
    text_res,
    gate_acc,
    gate_out,
    gate_in,
    gate_all,
    attn_ss,
    attn_rs,
    col_ss,
    col_rs,
    row_ss,
    row_rs,
    text_ss,
    text_rs,
    gather_ss,
    gather_rs,
    gate_ss,
    gate_rs,
    all_ss,
    all_rs,
):
    heads = part_ref.shape[0]
    device = lax.axis_index("seq")
    mine = lax.axis_index("head")
    row = device // COLS
    col = device % COLS
    bits = seq_count.bit_length() - 1
    text, width = dtk_ref.shape
    seg = 2 * text // seq_count
    far_rows = [dr for dr in row_deltas if dr != 0]

    def seq_id(index):
        return (index, mine)

    def head_id(index):
        return (device, index)

    col_to = {dc: neighbour(row, col, 0, dc, row_count if row_count == 2 else 1 << 20) for dc in (-1, 1)}
    row_to = {}
    for dr in far_rows:
        index, ok = neighbour(row, col, dr, 0, row_count)
        row_to[dr] = (index, None if row_count == 2 else ok)
    row_from = {dr: row_to[dr if row_count == 2 else -dr] for dr in far_rows}
    friends = [(seq_id(col_to[dc][0]), col_to[dc][1]) for dc in (-1, 1)]
    friends += [(seq_id(row_to[dr][0]), row_to[dr][1]) for dr in far_rows]
    partner_at = []
    bit_at = []
    for b in range(bits):
        bit = (device // (1 << b)) % 2
        bit_at.append(bit)
        partner_at.append(device + (1 - 2 * bit) * (1 << b))
    friends += [(seq_id(p), None) for p in partner_at]
    peers = [(mine + step) % head_count for step in range(1, head_count)]
    friends += [(head_id(p), None) for p in peers]
    greet(friends)

    order = far_rows + [0]
    chunks = [(h, k) for h in range(heads) for k in range(2)]
    col_copies = {}
    for dr in order:
        ri = row_deltas.index(dr)
        for h, k in chunks:
            for side, dc in ((0, -1), (1, 1)):
                target, ok = col_to[dc]
                copy = pltpu.make_async_remote_copy(
                    src_ref=part_ref.at[h, ri * 3 + 1 + side, k],
                    dst_ref=col_in.at[side, ri, h, k],
                    send_sem=col_ss.at[side, ri, h, k],
                    recv_sem=col_rs.at[side, ri, h, k],
                    device_id=seq_id(target),
                    device_id_type=MESH,
                )
                col_copies[dr, h, k, side] = (copy, ok)
                guarded(ok, copy.start)
    attn_copies = []
    for step in range(1, head_count):
        copy = pltpu.make_async_remote_copy(
            src_ref=attn_ref,
            dst_ref=attn_in.at[step - 1],
            send_sem=attn_ss.at[step - 1],
            recv_sem=attn_rs.at[step - 1],
            device_id=head_id(peers[step - 1]),
            device_id_type=MESH,
        )
        copy.start()
        attn_copies.append(copy)

    per = text // seg
    for i in range(per):
        acc[i] = dtk_ref[i * seg : (i + 1) * seg, :]
        acc[per + i] = dtv_ref[i * seg : (i + 1) * seg, :]

    def col_sum(dr, h, k):
        ri = row_deltas.index(dr)
        total = part_ref[h, ri * 3, k].astype(F32)
        for side, dc in ((0, -1), (1, 1)):
            came = col_to[-dc][1]
            copy, _ = col_copies[dr, h, k, side]
            guarded(came, copy.wait_recv)
            got = col_in[side, ri, h, k].astype(F32)
            total = total + jnp.where(came, got, 0.0)
        return total

    row_copies = []
    for fi, dr in enumerate(far_rows):
        for h, k in chunks:
            row_out[fi, h, k] = col_sum(dr, h, k).astype(BF16)
            target, ok = row_to[dr]
            copy = pltpu.make_async_remote_copy(
                src_ref=row_out.at[fi, h, k],
                dst_ref=row_in.at[fi, h, k],
                send_sem=row_ss.at[fi, h, k],
                recv_sem=row_rs.at[fi, h, k],
                device_id=seq_id(target),
                device_id_type=MESH,
            )
            guarded(ok, copy.start)
            row_copies.append((fi, dr, h, k, copy, ok))

    pending = []
    starts = [0]

    def halve(b):
        n = seq_count >> (b + 1)
        at = starts[-1]
        keep = at + bit_at[b] * n
        give = at + (1 - bit_at[b]) * n
        text_out[pl.ds(n, n)] = acc[pl.ds(give, n)].astype(BF16)
        copy = pltpu.make_async_remote_copy(
            src_ref=text_out.at[pl.ds(n, n)],
            dst_ref=text_in.at[pl.ds(n, n)],
            send_sem=text_ss.at[b],
            recv_sem=text_rs.at[b],
            device_id=seq_id(partner_at[b]),
            device_id_type=MESH,
        )
        copy.start()
        pending.append(copy)
        starts.append(keep)
        return copy, keep, n

    def finish(state):
        copy, keep, n = state
        copy.wait_recv()
        acc[pl.ds(keep, n)] = acc[pl.ds(keep, n)] + text_in[pl.ds(n, n)].astype(F32)

    state = halve(0)

    for copy in attn_copies:
        copy.wait_recv()
    cols = grad_ref.shape[1]
    piece = 384 if cols % 384 == 0 else 128
    for c in range(cols // piece):
        at = slice(c * piece, (c + 1) * piece)
        total = jnp.dot(attn_ref[...], w_ref[0, :, at], preferred_element_type=F32)
        for step in range(1, head_count):
            total = total + jnp.dot(
                attn_in[step - 1], w_ref[step, :, at], preferred_element_type=F32
            )
        gate_acc[:, at] = jnp.sum(grad_ref[:, at].astype(F32) * total, axis=0, keepdims=True)

    gate_copies = []

    def gate_send(b):
        gate_out[b] = gate_acc[...]
        copy = pltpu.make_async_remote_copy(
            src_ref=gate_out.at[b],
            dst_ref=gate_in.at[b],
            send_sem=gate_ss.at[b],
            recv_sem=gate_rs.at[b],
            device_id=seq_id(partner_at[b]),
            device_id_type=MESH,
        )
        copy.start()
        gate_copies.append(copy)

    def gate_take(b):
        gate_copies[b].wait_recv()
        gate_acc[...] = gate_acc[...] + gate_in[b]

    for b in range(bits):
        gate_send(b)
        finish(state)
        if b + 1 < bits:
            state = halve(b + 1)
        gate_take(b)

    all_copies = []
    gate_all[mine] = gate_acc[...]
    for step in range(1, head_count):
        copy = pltpu.make_async_remote_copy(
            src_ref=gate_acc,
            dst_ref=gate_all.at[mine],
            send_sem=all_ss.at[step - 1],
            recv_sem=all_rs.at[step - 1],
            device_id=head_id(peers[step - 1]),
            device_id_type=MESH,
        )
        copy.start()
        all_copies.append(copy)

    base = starts[-1]
    text_res[pl.ds(base, 1)] = acc[pl.ds(base, 1)].astype(BF16)
    for b in reversed(range(bits)):
        n = seq_count >> (b + 1)
        at = starts[b + 1]
        copy = pltpu.make_async_remote_copy(
            src_ref=text_res.at[pl.ds(at, n)],
            dst_ref=text_res.at[pl.ds(at, n)],
            send_sem=gather_ss.at[b],
            recv_sem=gather_rs.at[b],
            device_id=seq_id(partner_at[b]),
            device_id_type=MESH,
        )
        copy.start()
        pending.append(copy)
        copy.wait_recv()
    for i in range(per):
        tk_ref[i * seg : (i + 1) * seg, :] = text_res[i]
        tv_ref[i * seg : (i + 1) * seg, :] = text_res[per + i]

    cosine = cos_ref[...]
    sine = sin_ref[...]
    for h, k in chunks:
        total = col_sum(0, h, k)
        for fi, dr, ch, ck, copy, ok in row_copies:
            if (ch, ck) == (h, k):
                came = row_from[dr][1]
                guarded(came, copy.wait_recv)
                got = row_in[fi, h, k].astype(F32)
                total = total + (got if came is None else jnp.where(came, got, 0.0))
        at = slice(h * HEAD_DIM, (h + 1) * HEAD_DIM)
        if k == 0:
            dk_ref[:, at] = (total * cosine - partner(total) * sine).astype(BF16)
        else:
            dv_ref[:, at] = total.astype(BF16)

    for copy in all_copies:
        copy.wait_recv()
    for i in range(head_count):
        gate_ref[:, i * cols : (i + 1) * cols] = gate_all[i]

    for copy, ok in col_copies.values():
        guarded(ok, copy.wait_send)
    for fi, dr, h, k, copy, ok in row_copies:
        guarded(ok, copy.wait_send)
    for copy in attn_copies + pending + gate_copies + all_copies:
        copy.wait_send()


def shift(array, dr, dc, row_count):
    pairs = []
    for r in range(row_count):
        for c in range(COLS):
            to_r, to_c = r + dr, c + dc
            if row_count == 2:
                to_r = to_r % 2
            if 0 <= to_r < row_count and 0 <= to_c < COLS:
                pairs.append((r * COLS + c, to_r * COLS + to_c))
    return lax.ppermute(array, "seq", pairs)


def on_device(
    query_in,
    key_in,
    value_in,
    text_keys,
    text_values,
    text_mask,
    window_reach,
    tile_map,
    out_weight,
    gate_scale,
    grad_out,
):
    tile, width = query_in.shape
    heads = width // HEAD_DIM
    text = text_keys.shape[0]
    seq_count = lax.axis_size("seq")
    head_count = lax.axis_size("head")
    row_count = seq_count // COLS
    device = lax.axis_index("seq")
    mine = lax.axis_index("head")
    my_cols = grad_out.shape[1]
    vmem = pl.BlockSpec(memory_space=pltpu.VMEM)
    smem = pl.BlockSpec(memory_space=pltpu.SMEM)

    q_rot, kv, cosine, sine = pl.pallas_call(
        functools.partial(prep_kernel, heads),
        out_shape=(
            jax.ShapeDtypeStruct((tile, width), BF16),
            jax.ShapeDtypeStruct((2, tile, width), BF16),
            jax.ShapeDtypeStruct((tile, HEAD_DIM), F32),
            jax.ShapeDtypeStruct((tile, HEAD_DIM), F32),
        ),
        in_specs=[smem, vmem, vmem, vmem, vmem],
        out_specs=(vmem, vmem, vmem, vmem),
    )(tile_map, jnp.asarray(lane_tables()), query_in, key_in, value_in)

    row_deltas = (0,) if row_count == 1 else (0, 1) if row_count == 2 else (0, -1, 1)
    deltas = [(dr, dc) for dr in row_deltas for dc in (0, -1, 1)]
    by_row = {dr: kv if dr == 0 else shift(kv, -dr, 0, row_count) for dr in row_deltas}
    fetched = [by_row[dr] if dc == 0 else shift(by_row[dr], 0, -dc, row_count) for dr, dc in deltas]

    core = device % 2
    half = width // 2
    rows = [None] * head_count
    own_cols = lax.dynamic_slice_in_dim(out_weight, mine * my_cols, my_cols, 1)
    pieces = [own_cols]
    swap = [(i, i ^ 1) for i in range(seq_count)]
    for step in range(1, head_count):
        to = (mine + step) % head_count
        block = lax.dynamic_slice(out_weight, (core * half, to * my_cols), (half, my_cols))
        ring = [(i, (i + step) % head_count) for i in range(head_count)]
        got = lax.ppermute(block, "head", ring)
        other = lax.ppermute(got, "seq", swap)
        pieces.append(
            jnp.concatenate(
                [jnp.where(core == 0, got, other), jnp.where(core == 0, other, got)], axis=0
            )
        )
    grad_f = grad_out.astype(F32)
    gate_cols = lax.dynamic_slice_in_dim(gate_scale, mine * my_cols, my_cols, 0)
    grad_proj = (grad_f * gate_cols[None, :]).astype(BF16)
    total = lax.dot_general(grad_proj, pieces[0], (((1,), (1,)), ((), ())), preferred_element_type=F32)
    for step in range(1, head_count):
        part = lax.dot_general(
            grad_proj, pieces[step], (((1,), (1,)), ((), ())), preferred_element_type=F32
        ).astype(BF16)
        back = [(i, (i - step) % head_count) for i in range(head_count)]
        total = total + lax.ppermute(part, "head", back).astype(F32)
    grad_attn = total.astype(BF16)

    nb = len(deltas)
    blocks = jnp.stack(fetched)
    head_spec = pl.BlockSpec((tile, HEAD_DIM), lambda h: (0, h))
    text_spec = pl.BlockSpec((text, HEAD_DIM), lambda h: (0, h))
    block_spec = pl.BlockSpec((nb, 2, tile, HEAD_DIM), lambda h: (0, 0, 0, h))
    part_spec = pl.BlockSpec((1, nb, 2, tile, HEAD_DIM), lambda h: (h, 0, 0, 0, 0))
    table_spec = pl.BlockSpec((tile, HEAD_DIM), lambda h: (0, 0))
    attn, grad_query, partials, text_key_grad, text_value_grad = pl.pallas_call(
        functools.partial(attend_kernel, deltas, row_count),
        grid=(heads,),
        out_shape=(
            jax.ShapeDtypeStruct((tile, width), BF16),
            jax.ShapeDtypeStruct((tile, width), BF16),
            jax.ShapeDtypeStruct((heads, nb, 2, tile, HEAD_DIM), BF16),
            jax.ShapeDtypeStruct((text, width), F32),
            jax.ShapeDtypeStruct((text, width), F32),
        ),
        in_specs=[
            smem,
            pl.BlockSpec((text, 1), lambda h: (0, 0)),
            head_spec,
            head_spec,
            block_spec,
            text_spec,
            text_spec,
            table_spec,
            table_spec,
        ],
        out_specs=(head_spec, head_spec, part_spec, text_spec, text_spec),
        scratch_shapes=[
            pltpu.VMEM((nb * tile + text, tile), F32),
            pltpu.VMEM((1, tile), F32),
            pltpu.VMEM((1, tile), F32),
            pltpu.VMEM((HEAD_DIM, tile), F32),
            pltpu.VMEM((HEAD_DIM, tile), F32),
        ],
        compiler_params=pltpu.CompilerParams(vmem_limit_bytes=48 * 1024 * 1024),
    )(
        window_reach,
        text_mask[:, None],
        q_rot,
        grad_attn,
        blocks,
        text_keys,
        text_values,
        cosine,
        sine,
    )

    nr = len(row_deltas)
    nf = max(nr - 1, 1)
    bits = seq_count.bit_length() - 1
    seg = 2 * text // seq_count
    peers = max(head_count - 1, 1)
    dma = pltpu.SemaphoreType.DMA
    grad_key, grad_value, text_key_sum, text_value_sum, grad_gate = pl.pallas_call(
        functools.partial(tail_kernel, row_deltas, row_count, seq_count, head_count),
        out_shape=(
            jax.ShapeDtypeStruct((tile, width), BF16),
            jax.ShapeDtypeStruct((tile, width), BF16),
            jax.ShapeDtypeStruct((text, width), BF16),
            jax.ShapeDtypeStruct((text, width), BF16),
            jax.ShapeDtypeStruct((1, head_count * my_cols), F32),
        ),
        in_specs=[vmem] * 8,
        out_specs=(vmem,) * 5,
        scratch_shapes=[
            pltpu.VMEM((peers, tile, width), BF16),
            pltpu.VMEM((2, nr, heads, 2, tile, HEAD_DIM), BF16),
            pltpu.VMEM((nf, heads, 2, tile, HEAD_DIM), BF16),
            pltpu.VMEM((nf, heads, 2, tile, HEAD_DIM), BF16),
            pltpu.VMEM((seq_count, seg, width), F32),
            pltpu.VMEM((seq_count, seg, width), BF16),
            pltpu.VMEM((seq_count, seg, width), BF16),
            pltpu.VMEM((seq_count, seg, width), BF16),
            pltpu.VMEM((1, my_cols), F32),
            pltpu.VMEM((bits, 1, my_cols), F32),
            pltpu.VMEM((bits, 1, my_cols), F32),
            pltpu.VMEM((head_count, 1, my_cols), F32),
            dma((peers,)),
            dma((peers,)),
            dma((2, nr, heads, 2)),
            dma((2, nr, heads, 2)),
            dma((nf, heads, 2)),
            dma((nf, heads, 2)),
            dma((bits,)),
            dma((bits,)),
            dma((bits,)),
            dma((bits,)),
            dma((bits,)),
            dma((bits,)),
            dma((peers,)),
            dma((peers,)),
        ],
        compiler_params=pltpu.CompilerParams(
            collective_id=1, has_side_effects=True, vmem_limit_bytes=48 * 1024 * 1024
        ),
    )(
        attn,
        partials,
        text_key_grad,
        text_value_grad,
        jnp.stack(pieces),
        grad_out,
        cosine,
        sine,
    )
    return (
        grad_query,
        grad_key,
        grad_value,
        text_key_sum,
        text_value_sum,
        grad_gate.reshape(-1),
    )


def solution(mesh):
    placed = (
        P("seq", "head"),
        P("seq", "head"),
        P("seq", "head"),
        P(None, "head"),
        P(None, "head"),
        P(),
        P("head", None),
        P(),
        P("head", None),
        P(),
        P("seq", "head"),
    )
    return jax.shard_map(
        on_device,
        mesh=mesh,
        in_specs=placed,
        out_specs=(
            P("seq", "head"),
            P("seq", "head"),
            P("seq", "head"),
            P(None, "head"),
            P(None, "head"),
            P(),
        ),
        check_vma=False,
    )
```

```python
import functools

import jax
import jax.numpy as jnp
import numpy as np
from jax import lax
from jax.experimental import pallas as pl
from jax.experimental.pallas import tpu as pltpu
from jax.sharding import PartitionSpec as P

HEAD_DIM = 128
TILE_T = 6
TILE_H = 8
TILE_W = 8
COLS = 8
THETA = 256.0
NEG = -1e30
F32 = jnp.float32
BF16 = jnp.bfloat16
MESH = pl.DeviceIdType.MESH


def lane_tables():
    first = HEAD_DIM // 8
    second = (HEAD_DIM - first) // 2
    freqs = np.zeros((HEAD_DIM,), np.float32)
    section = np.zeros((HEAD_DIM,), np.float32)
    sign = np.zeros((HEAD_DIM,), np.float32)
    offset = 0
    for number, length in enumerate((first, second, second)):
        half = length // 2
        f = (THETA ** (-2.0 * np.arange(half) / length)).astype(np.float32)
        freqs[offset : offset + half] = f
        freqs[offset + half : offset + length] = f
        section[offset : offset + length] = number
        sign[offset : offset + half] = -1.0
        sign[offset + half : offset + length] = 1.0
        offset += length
    return np.stack([freqs, section, sign] + [np.zeros_like(freqs)] * 5)


def partner(x):
    first = HEAD_DIM // 8
    second = (HEAD_DIM - first) // 2
    lane = lax.broadcasted_iota(jnp.int32, x.shape, 1)
    a = first // 2
    b = second // 2
    up_a = pltpu.roll(x, HEAD_DIM - a, 1)
    down_a = pltpu.roll(x, a, 1)
    up_b = pltpu.roll(x, HEAD_DIM - b, 1)
    down_b = pltpu.roll(x, b, 1)
    in_a = jnp.where(lane < a, up_a, down_a)
    is_first = (lane < first + b) | ((lane >= first + second) & (lane < first + second + b))
    in_b = jnp.where(is_first, up_b, down_b)
    return jnp.where(lane < first, in_a, in_b)


def neighbour(row, col, dr, dc, row_count):
    to_r, to_c = row + dr, col + dc
    ok = (to_c >= 0) & (to_c < COLS)
    if row_count == 2:
        to_r = (to_r + 2) % 2
    else:
        ok = ok & (to_r >= 0) & (to_r < row_count)
    return to_r * COLS + to_c, ok


def greet(axis_devices):
    barrier = pltpu.get_barrier_semaphore()
    for target, ok in axis_devices:
        if ok is None:
            pl.semaphore_signal(barrier, inc=1, device_id=target, device_id_type=MESH)
        else:

            @pl.when(ok)
            def _():
                pl.semaphore_signal(barrier, inc=1, device_id=target, device_id_type=MESH)

    count = 0
    for _, ok in axis_devices:
        count = count + (1 if ok is None else ok.astype(jnp.int32))
    pl.semaphore_wait(barrier, count)


def guarded(ok, act):
    if ok is None:
        act()
    else:
        pl.when(ok)(act)


def head_kernel(
    row_deltas,
    row_count,
    head_count,
    tile_ref,
    lanes_ref,
    q_ref,
    k_ref,
    v_ref,
    w_ref,
    gate_ref,
    grad_ref,
    qr_ref,
    kv_ref,
    cos_ref,
    sin_ref,
    wall_ref,
    ga_ref,
    proj,
    part_out,
    part_in,
    row_ss,
    row_rs,
    col_ss,
    col_rs,
    w_ss,
    w_rs,
    swap_ss,
    swap_rs,
    part_ss,
    part_rs,
):
    heads = kv_ref.shape[0]
    device = lax.axis_index("seq")
    mine = lax.axis_index("head")
    row = device // COLS
    col = device % COLS
    core = device % 2
    width = q_ref.shape[1]
    half = width // 2
    my_cols = grad_ref.shape[1]
    far_rows = [dr for dr in row_deltas if dr != 0]

    def seq_id(index):
        return (index, mine)

    def head_id(index):
        return (device, index)

    col_to = {dc: neighbour(row, col, 0, dc, row_count if row_count == 2 else 1 << 20) for dc in (-1, 1)}
    row_to = {}
    for dr in far_rows:
        index, ok = neighbour(row, col, dr, 0, row_count)
        row_to[dr] = (index, None if row_count == 2 else ok)
    opposite = {dr: (dr if row_count == 2 else -dr) for dr in far_rows}
    sibling = device + 1 - 2 * core
    peers = [(mine + step) % head_count for step in range(1, head_count)]
    friends = [(seq_id(col_to[dc][0]), col_to[dc][1]) for dc in (-1, 1)]
    friends += [(seq_id(row_to[dr][0]), row_to[dr][1]) for dr in far_rows]
    friends += [(seq_id(sibling), None)]
    friends += [(head_id(p), None) for p in peers]
    greet(friends)

    def start(src, dst, ss, rs, target, ok):
        copy = pltpu.make_async_remote_copy(
            src_ref=src, dst_ref=dst, send_sem=ss, recv_sem=rs, device_id=target, device_id_type=MESH
        )
        guarded(ok, copy.start)
        return copy, ok

    sent = []
    row_copies = {}
    col_copies = {}

    def send_rows(src, h, k):
        for dr in far_rows:
            slot = row_deltas.index(opposite[dr])
            target, ok = row_to[dr]
            row_copies[slot, h, k] = start(
                src, kv_ref.at[h, slot * 3, k], row_ss.at[slot - 1, h, k], row_rs.at[slot - 1, h, k],
                seq_id(target), ok,
            )
            sent.append(row_copies[slot, h, k])

    def send_cols(src, ri, h, k, have):
        for side, dc in ((0, -1), (1, 1)):
            target, ok = col_to[dc]
            number = ri * 3 + (2 if dc == -1 else 1)
            if have is not None:
                ok = ok & have
            col_copies[side, ri, h, k] = start(
                src, kv_ref.at[h, number, k], col_ss.at[side, ri, h, k], col_rs.at[side, ri, h, k],
                seq_id(target), ok,
            )
            sent.append(col_copies[side, ri, h, k])

    def part_of(h):
        return slice(h * HEAD_DIM, (h + 1) * HEAD_DIM)

    for h in range(heads):
        send_rows(v_ref.at[:, part_of(h)], h, 1)
    w_copies = []
    rows_at = pl.ds(pl.multiple_of(core * half, half), half)
    for step in range(1, head_count):
        cols_at = pl.ds(pl.multiple_of(peers[step - 1] * my_cols, 128), my_cols)
        w_copies.append(
            start(
                w_ref.at[rows_at, cols_at], wall_ref.at[step, rows_at, :],
                w_ss.at[step - 1], w_rs.at[step - 1], head_id(peers[step - 1]), None,
            )
        )
    for h in range(heads):
        send_cols(v_ref.at[:, part_of(h)], 0, h, 1, None)

    freqs = lanes_ref[0:1, :]
    section = lanes_ref[1:2, :]
    sign = lanes_ref[2:3, :]

    def table(count, base):
        step = lax.broadcasted_iota(jnp.int32, (8, HEAD_DIM), 0)
        pos = (base * count + step).astype(F32)
        angle = pos * freqs
        return jnp.cos(angle), jnp.sin(angle) * sign

    cf, sf = table(TILE_T, tile_ref[device, 0])
    cr, sr = table(TILE_H, tile_ref[device, 1])
    cc, sc = table(TILE_W, tile_ref[device, 2])
    for t in range(TILE_T):
        for r in range(TILE_H):
            at = pl.ds((t * TILE_H + r) * TILE_W, TILE_W)
            for out, f, w, c in ((cos_ref, cf, cr, cc), (sin_ref, sf, sr, sc)):
                low = jnp.where(section == 0.0, f[t : t + 1, :], w[r : r + 1, :])
                full = jnp.broadcast_to(section, c.shape)
                out[at, :] = jnp.where(full < 2.0, jnp.broadcast_to(low, c.shape), c)
    cosine = cos_ref[...]
    sine = sin_ref[...]
    for h in range(heads):
        x = k_ref[:, part_of(h)].astype(F32)
        kv_ref[h, 0, 0] = (x * cosine + partner(x) * sine).astype(BF16)
        send_rows(kv_ref.at[h, 0, 0], h, 0)
        send_cols(kv_ref.at[h, 0, 0], 0, h, 0, None)
    for h in range(heads):
        x = q_ref[:, part_of(h)].astype(F32)
        qr_ref[:, part_of(h)] = (x * cosine + partner(x) * sine).astype(BF16)
        kv_ref[h, 0, 1] = v_ref[:, part_of(h)]

    own_at = pl.ds(pl.multiple_of(mine * my_cols, 128), my_cols)
    wall_ref[0] = w_ref[:, own_at]
    proj[...] = (grad_ref[...].astype(F32) * gate_ref[:, own_at]).astype(BF16)

    def times(step):
        return lax.dot_general(
            proj[...], wall_ref[step], (((1,), (1,)), ((), ())), preferred_element_type=F32
        )

    total = times(0)

    def forward(h, k):
        for dr in far_rows:
            slot = row_deltas.index(dr)
            have = row_to[dr][1]
            copy, _ = row_copies[slot, h, k]
            guarded(have, copy.wait_recv)
            send_cols(kv_ref.at[h, slot * 3, k], slot, h, k, have)

    for h in range(heads):
        forward(h, 1)
    swaps = []
    for step in range(1, head_count):
        w_copies[step - 1][0].wait_recv()
        swaps.append(
            start(
                wall_ref.at[step, rows_at, :], wall_ref.at[step, rows_at, :],
                swap_ss.at[step - 1], swap_rs.at[step - 1], seq_id(sibling), None,
            )
        )
    for h in range(heads - 1):
        forward(h, 0)
    parts = []
    for step in range(1, head_count):
        swaps[step - 1][0].wait_recv()
        part_out[step - 1] = times(step).astype(BF16)
        back = (mine + head_count - step) % head_count
        parts.append(
            start(
                part_out.at[step - 1], part_in.at[step - 1],
                part_ss.at[step - 1], part_rs.at[step - 1], head_id(back), None,
            )
        )
    forward(heads - 1, 0)
    for step in range(1, head_count):
        parts[step - 1][0].wait_recv()
        total = total + part_in[step - 1].astype(F32)
    ga_ref[...] = total.astype(BF16)

    for (side, ri, h, k), (copy, _) in col_copies.items():
        came = col_to[1 if side == 0 else -1][1]
        if ri > 0:
            have = row_to[row_deltas[ri]][1]
            if have is not None:
                came = came & have
        guarded(came, copy.wait_recv)
    for copy, ok in sent + w_copies + swaps + parts:
        guarded(ok, copy.wait_send)


def attend_kernel(
    deltas,
    row_count,
    reach_ref,
    mask_ref,
    q_ref,
    g_ref,
    kv_ref,
    tk_ref,
    tv_ref,
    cos_ref,
    sin_ref,
    attn_ref,
    dq_ref,
    part_ref,
    dtk_ref,
    dtv_ref,
    s_ref,
    m_ref,
    l_ref,
    o_ref,
    dqa_ref,
):
    head = pl.program_id(0)
    device = lax.axis_index("seq")
    row = device // COLS
    col = device % COLS
    tile = q_ref.shape[0]
    text = tk_ref.shape[0]
    scale = HEAD_DIM ** (-0.5)
    reach_r = reach_ref[head, 0]
    reach_c = reach_ref[head, 1]
    q = q_ref[...]
    g = g_ref[...]
    blocks = []
    for number, (dr, dc) in enumerate(deltas):
        ok = (abs(dr) <= reach_r) & (abs(dc) <= reach_c)
        ok = ok & (col + dc >= 0) & (col + dc < COLS)
        if row_count > 2:
            ok = ok & (row + dr >= 0) & (row + dr < row_count)
        blocks.append((number, ok))
    nb = len(deltas)
    text_at = slice(nb * tile, nb * tile + text)

    def nt(a, b):
        return lax.dot_general(a, b, (((1,), (1,)), ((), ())), preferred_element_type=F32)

    def tn(a, b):
        return lax.dot_general(a, b, (((0,), (0,)), ((), ())), preferred_element_type=F32)

    def nn(a, b):
        return lax.dot_general(a, b, (((1,), (0,)), ((), ())), preferred_element_type=F32)

    s = nt(tk_ref[...], q) * scale
    s = jnp.where(mask_ref[...] == 1, s, NEG)
    s_ref[text_at, :] = s
    m_ref[...] = jnp.max(s, axis=0, keepdims=True)
    for number, ok in blocks:
        at = slice(number * tile, (number + 1) * tile)

        @pl.when(ok)
        def _():
            s = nt(kv_ref[0, number, 0], q) * scale
            s_ref[at, :] = s
            m_ref[...] = jnp.maximum(m_ref[...], jnp.max(s, axis=0, keepdims=True))

    e = jnp.exp(s_ref[text_at, :] - m_ref[...])
    s_ref[text_at, :] = e
    l_ref[...] = jnp.sum(e, axis=0, keepdims=True)
    for number, ok in blocks:
        at = slice(number * tile, (number + 1) * tile)

        @pl.when(ok)
        def _():
            e = jnp.exp(s_ref[at, :] - m_ref[...])
            s_ref[at, :] = e
            l_ref[...] += jnp.sum(e, axis=0, keepdims=True)

    inv = 1.0 / l_ref[...]
    l_ref[...] = inv
    p = (s_ref[text_at, :] * inv).astype(BF16)
    o_ref[...] = tn(tv_ref[...], p)
    dtv_ref[...] = nn(p, g)
    for number, ok in blocks:
        at = slice(number * tile, (number + 1) * tile)

        @pl.when(ok)
        def _():
            p = (s_ref[at, :] * l_ref[...]).astype(BF16)
            o_ref[...] += tn(kv_ref[0, number, 1], p)
            part_ref[0, number, 1] = nn(p, g).astype(BF16)

        @pl.when(jnp.logical_not(ok))
        def _():
            part_ref[0, number] = jnp.zeros(part_ref.shape[2:], BF16)

    attn = o_ref[...].T.astype(BF16)
    attn_ref[...] = attn
    delta_rows = g.astype(F32) * attn.astype(F32)
    delta = jnp.sum(delta_rows.T, axis=0, keepdims=True)
    m_ref[...] = delta
    ds = (s_ref[text_at, :] * l_ref[...] * (nt(tv_ref[...], g) - delta)).astype(BF16)
    dqa_ref[...] = tn(tk_ref[...], ds)
    dtk_ref[...] = nn(ds, q) * scale
    for number, ok in blocks:
        at = slice(number * tile, (number + 1) * tile)

        @pl.when(ok)
        def _():
            dp = nt(kv_ref[0, number, 1], g)
            ds = (s_ref[at, :] * l_ref[...] * (dp - m_ref[...])).astype(BF16)
            dqa_ref[...] += tn(kv_ref[0, number, 0], ds)
            part_ref[0, number, 0] = (nn(ds, q) * scale).astype(BF16)

    dq = dqa_ref[...].T * scale
    dq_ref[...] = (dq * cos_ref[...] - partner(dq) * sin_ref[...]).astype(BF16)


def tail_kernel(
    row_deltas,
    row_count,
    seq_count,
    head_count,
    attn_ref,
    part_ref,
    dtk_ref,
    dtv_ref,
    w_ref,
    grad_ref,
    cos_ref,
    sin_ref,
    dk_ref,
    dv_ref,
    tk_ref,
    tv_ref,
    gate_ref,
    attn_in,
    col_in,
    row_out,
    row_in,
    acc,
    text_out,
    text_in,
    text_res,
    gate_acc,
    gate_out,
    gate_in,
    gate_all,
    attn_ss,
    attn_rs,
    col_ss,
    col_rs,
    row_ss,
    row_rs,
    text_ss,
    text_rs,
    gather_ss,
    gather_rs,
    gate_ss,
    gate_rs,
    all_ss,
    all_rs,
):
    heads = part_ref.shape[0]
    device = lax.axis_index("seq")
    mine = lax.axis_index("head")
    row = device // COLS
    col = device % COLS
    bits = seq_count.bit_length() - 1
    text, width = dtk_ref.shape
    seg = 2 * text // seq_count
    far_rows = [dr for dr in row_deltas if dr != 0]

    def seq_id(index):
        return (index, mine)

    def head_id(index):
        return (device, index)

    col_to = {dc: neighbour(row, col, 0, dc, row_count if row_count == 2 else 1 << 20) for dc in (-1, 1)}
    row_to = {}
    for dr in far_rows:
        index, ok = neighbour(row, col, dr, 0, row_count)
        row_to[dr] = (index, None if row_count == 2 else ok)
    row_from = {dr: row_to[dr if row_count == 2 else -dr] for dr in far_rows}
    friends = [(seq_id(col_to[dc][0]), col_to[dc][1]) for dc in (-1, 1)]
    friends += [(seq_id(row_to[dr][0]), row_to[dr][1]) for dr in far_rows]
    partner_at = []
    bit_at = []
    for b in range(bits):
        bit = (device // (1 << b)) % 2
        bit_at.append(bit)
        partner_at.append(device + (1 - 2 * bit) * (1 << b))
    friends += [(seq_id(p), None) for p in partner_at]
    peers = [(mine + step) % head_count for step in range(1, head_count)]
    friends += [(head_id(p), None) for p in peers]
    greet(friends)

    order = far_rows + [0]
    chunks = [(h, k) for h in range(heads) for k in range(2)]
    col_copies = {}
    for dr in order:
        ri = row_deltas.index(dr)
        for h, k in chunks:
            for side, dc in ((0, -1), (1, 1)):
                target, ok = col_to[dc]
                copy = pltpu.make_async_remote_copy(
                    src_ref=part_ref.at[h, ri * 3 + 1 + side, k],
                    dst_ref=col_in.at[side, ri, h, k],
                    send_sem=col_ss.at[side, ri, h, k],
                    recv_sem=col_rs.at[side, ri, h, k],
                    device_id=seq_id(target),
                    device_id_type=MESH,
                )
                col_copies[dr, h, k, side] = (copy, ok)
                guarded(ok, copy.start)
    attn_copies = []
    for step in range(1, head_count):
        copy = pltpu.make_async_remote_copy(
            src_ref=attn_ref,
            dst_ref=attn_in.at[step - 1],
            send_sem=attn_ss.at[step - 1],
            recv_sem=attn_rs.at[step - 1],
            device_id=head_id(peers[step - 1]),
            device_id_type=MESH,
        )
        copy.start()
        attn_copies.append(copy)

    per = text // seg
    for i in range(per):
        acc[i] = dtk_ref[i * seg : (i + 1) * seg, :]
        acc[per + i] = dtv_ref[i * seg : (i + 1) * seg, :]

    def col_sum(dr, h, k):
        ri = row_deltas.index(dr)
        total = part_ref[h, ri * 3, k].astype(F32)
        for side, dc in ((0, -1), (1, 1)):
            came = col_to[-dc][1]
            copy, _ = col_copies[dr, h, k, side]
            guarded(came, copy.wait_recv)
            got = col_in[side, ri, h, k].astype(F32)
            total = total + jnp.where(came, got, 0.0)
        return total

    row_copies = []
    for fi, dr in enumerate(far_rows):
        for h, k in chunks:
            row_out[fi, h, k] = col_sum(dr, h, k).astype(BF16)
            target, ok = row_to[dr]
            copy = pltpu.make_async_remote_copy(
                src_ref=row_out.at[fi, h, k],
                dst_ref=row_in.at[fi, h, k],
                send_sem=row_ss.at[fi, h, k],
                recv_sem=row_rs.at[fi, h, k],
                device_id=seq_id(target),
                device_id_type=MESH,
            )
            guarded(ok, copy.start)
            row_copies.append((fi, dr, h, k, copy, ok))

    pending = []
    starts = [0]

    def halve(b):
        n = seq_count >> (b + 1)
        at = starts[-1]
        keep = at + bit_at[b] * n
        give = at + (1 - bit_at[b]) * n
        text_out[pl.ds(n, n)] = acc[pl.ds(give, n)].astype(BF16)
        copy = pltpu.make_async_remote_copy(
            src_ref=text_out.at[pl.ds(n, n)],
            dst_ref=text_in.at[pl.ds(n, n)],
            send_sem=text_ss.at[b],
            recv_sem=text_rs.at[b],
            device_id=seq_id(partner_at[b]),
            device_id_type=MESH,
        )
        copy.start()
        pending.append(copy)
        starts.append(keep)
        return copy, keep, n

    def finish(state):
        copy, keep, n = state
        copy.wait_recv()
        acc[pl.ds(keep, n)] = acc[pl.ds(keep, n)] + text_in[pl.ds(n, n)].astype(F32)

    state = halve(0)

    for copy in attn_copies:
        copy.wait_recv()
    cols = grad_ref.shape[1]
    piece = 384 if cols % 384 == 0 else 128
    for c in range(cols // piece):
        at = slice(c * piece, (c + 1) * piece)
        total = jnp.dot(attn_ref[...], w_ref[0, :, at], preferred_element_type=F32)
        for step in range(1, head_count):
            total = total + jnp.dot(
                attn_in[step - 1], w_ref[step, :, at], preferred_element_type=F32
            )
        gate_acc[:, at] = jnp.sum(grad_ref[:, at].astype(F32) * total, axis=0, keepdims=True)

    gate_copies = []

    def gate_send(b):
        gate_out[b] = gate_acc[...]
        copy = pltpu.make_async_remote_copy(
            src_ref=gate_out.at[b],
            dst_ref=gate_in.at[b],
            send_sem=gate_ss.at[b],
            recv_sem=gate_rs.at[b],
            device_id=seq_id(partner_at[b]),
            device_id_type=MESH,
        )
        copy.start()
        gate_copies.append(copy)

    def gate_take(b):
        gate_copies[b].wait_recv()
        gate_acc[...] = gate_acc[...] + gate_in[b]

    for b in range(bits):
        gate_send(b)
        finish(state)
        if b + 1 < bits:
            state = halve(b + 1)
        gate_take(b)

    all_copies = []
    gate_all[mine] = gate_acc[...]
    for step in range(1, head_count):
        copy = pltpu.make_async_remote_copy(
            src_ref=gate_acc,
            dst_ref=gate_all.at[mine],
            send_sem=all_ss.at[step - 1],
            recv_sem=all_rs.at[step - 1],
            device_id=head_id(peers[step - 1]),
            device_id_type=MESH,
        )
        copy.start()
        all_copies.append(copy)

    base = starts[-1]
    text_res[pl.ds(base, 1)] = acc[pl.ds(base, 1)].astype(BF16)
    for b in reversed(range(bits)):
        n = seq_count >> (b + 1)
        at = starts[b + 1]
        copy = pltpu.make_async_remote_copy(
            src_ref=text_res.at[pl.ds(at, n)],
            dst_ref=text_res.at[pl.ds(at, n)],
            send_sem=gather_ss.at[b],
            recv_sem=gather_rs.at[b],
            device_id=seq_id(partner_at[b]),
            device_id_type=MESH,
        )
        copy.start()
        pending.append(copy)
        copy.wait_recv()
    for i in range(per):
        tk_ref[i * seg : (i + 1) * seg, :] = text_res[i]
        tv_ref[i * seg : (i + 1) * seg, :] = text_res[per + i]

    cosine = cos_ref[...]
    sine = sin_ref[...]
    for h, k in chunks:
        total = col_sum(0, h, k)
        for fi, dr, ch, ck, copy, ok in row_copies:
            if (ch, ck) == (h, k):
                came = row_from[dr][1]
                guarded(came, copy.wait_recv)
                got = row_in[fi, h, k].astype(F32)
                total = total + (got if came is None else jnp.where(came, got, 0.0))
        at = slice(h * HEAD_DIM, (h + 1) * HEAD_DIM)
        if k == 0:
            dk_ref[:, at] = (total * cosine - partner(total) * sine).astype(BF16)
        else:
            dv_ref[:, at] = total.astype(BF16)

    for copy in all_copies:
        copy.wait_recv()
    for i in range(head_count):
        gate_ref[:, i * cols : (i + 1) * cols] = gate_all[i]

    for copy, ok in col_copies.values():
        guarded(ok, copy.wait_send)
    for fi, dr, h, k, copy, ok in row_copies:
        guarded(ok, copy.wait_send)
    for copy in attn_copies + pending + gate_copies + all_copies:
        copy.wait_send()


def on_device(
    query_in,
    key_in,
    value_in,
    text_keys,
    text_values,
    text_mask,
    window_reach,
    tile_map,
    out_weight,
    gate_scale,
    grad_out,
):
    tile, width = query_in.shape
    heads = width // HEAD_DIM
    text = text_keys.shape[0]
    seq_count = lax.axis_size("seq")
    head_count = lax.axis_size("head")
    row_count = seq_count // COLS
    my_cols = grad_out.shape[1]
    vmem = pl.BlockSpec(memory_space=pltpu.VMEM)
    smem = pl.BlockSpec(memory_space=pltpu.SMEM)

    row_deltas = (0,) if row_count == 1 else (0, 1) if row_count == 2 else (0, -1, 1)
    deltas = [(dr, dc) for dr in row_deltas for dc in (0, -1, 1)]
    nb = len(deltas)
    nr = len(row_deltas)
    nf = max(nr - 1, 1)
    peers = max(head_count - 1, 1)
    dma = pltpu.SemaphoreType.DMA
    q_rot, blocks, cosine, sine, pieces, grad_attn = pl.pallas_call(
        functools.partial(head_kernel, row_deltas, row_count, head_count),
        out_shape=(
            jax.ShapeDtypeStruct((tile, width), BF16),
            jax.ShapeDtypeStruct((heads, nb, 2, tile, HEAD_DIM), BF16),
            jax.ShapeDtypeStruct((tile, HEAD_DIM), F32),
            jax.ShapeDtypeStruct((tile, HEAD_DIM), F32),
            jax.ShapeDtypeStruct((head_count, width, my_cols), BF16),
            jax.ShapeDtypeStruct((tile, width), BF16),
        ),
        in_specs=[smem] + [vmem] * 7,
        out_specs=(vmem,) * 6,
        scratch_shapes=[
            pltpu.VMEM((tile, my_cols), BF16),
            pltpu.VMEM((peers, tile, width), BF16),
            pltpu.VMEM((peers, tile, width), BF16),
            dma((nf, heads, 2)),
            dma((nf, heads, 2)),
            dma((2, nr, heads, 2)),
            dma((2, nr, heads, 2)),
            dma((peers,)),
            dma((peers,)),
            dma((peers,)),
            dma((peers,)),
            dma((peers,)),
            dma((peers,)),
        ],
        compiler_params=pltpu.CompilerParams(
            collective_id=0, has_side_effects=True, vmem_limit_bytes=48 * 1024 * 1024
        ),
    )(
        tile_map,
        jnp.asarray(lane_tables()),
        query_in,
        key_in,
        value_in,
        out_weight,
        gate_scale[None, :],
        grad_out,
    )

    head_spec = pl.BlockSpec((tile, HEAD_DIM), lambda h: (0, h))
    text_spec = pl.BlockSpec((text, HEAD_DIM), lambda h: (0, h))
    part_spec = pl.BlockSpec((1, nb, 2, tile, HEAD_DIM), lambda h: (h, 0, 0, 0, 0))
    table_spec = pl.BlockSpec((tile, HEAD_DIM), lambda h: (0, 0))
    attn, grad_query, partials, text_key_grad, text_value_grad = pl.pallas_call(
        functools.partial(attend_kernel, deltas, row_count),
        grid=(heads,),
        out_shape=(
            jax.ShapeDtypeStruct((tile, width), BF16),
            jax.ShapeDtypeStruct((tile, width), BF16),
            jax.ShapeDtypeStruct((heads, nb, 2, tile, HEAD_DIM), BF16),
            jax.ShapeDtypeStruct((text, width), F32),
            jax.ShapeDtypeStruct((text, width), F32),
        ),
        in_specs=[
            smem,
            pl.BlockSpec((text, 1), lambda h: (0, 0)),
            head_spec,
            head_spec,
            part_spec,
            text_spec,
            text_spec,
            table_spec,
            table_spec,
        ],
        out_specs=(head_spec, head_spec, part_spec, text_spec, text_spec),
        scratch_shapes=[
            pltpu.VMEM((nb * tile + text, tile), F32),
            pltpu.VMEM((1, tile), F32),
            pltpu.VMEM((1, tile), F32),
            pltpu.VMEM((HEAD_DIM, tile), F32),
            pltpu.VMEM((HEAD_DIM, tile), F32),
        ],
        compiler_params=pltpu.CompilerParams(vmem_limit_bytes=48 * 1024 * 1024),
    )(
        window_reach,
        text_mask[:, None],
        q_rot,
        grad_attn,
        blocks,
        text_keys,
        text_values,
        cosine,
        sine,
    )

    bits = seq_count.bit_length() - 1
    seg = 2 * text // seq_count
    grad_key, grad_value, text_key_sum, text_value_sum, grad_gate = pl.pallas_call(
        functools.partial(tail_kernel, row_deltas, row_count, seq_count, head_count),
        out_shape=(
            jax.ShapeDtypeStruct((tile, width), BF16),
            jax.ShapeDtypeStruct((tile, width), BF16),
            jax.ShapeDtypeStruct((text, width), BF16),
            jax.ShapeDtypeStruct((text, width), BF16),
            jax.ShapeDtypeStruct((1, head_count * my_cols), F32),
        ),
        in_specs=[vmem] * 8,
        out_specs=(vmem,) * 5,
        scratch_shapes=[
            pltpu.VMEM((peers, tile, width), BF16),
            pltpu.VMEM((2, nr, heads, 2, tile, HEAD_DIM), BF16),
            pltpu.VMEM((nf, heads, 2, tile, HEAD_DIM), BF16),
            pltpu.VMEM((nf, heads, 2, tile, HEAD_DIM), BF16),
            pltpu.VMEM((seq_count, seg, width), F32),
            pltpu.VMEM((seq_count, seg, width), BF16),
            pltpu.VMEM((seq_count, seg, width), BF16),
            pltpu.VMEM((seq_count, seg, width), BF16),
            pltpu.VMEM((1, my_cols), F32),
            pltpu.VMEM((bits, 1, my_cols), F32),
            pltpu.VMEM((bits, 1, my_cols), F32),
            pltpu.VMEM((head_count, 1, my_cols), F32),
            dma((peers,)),
            dma((peers,)),
            dma((2, nr, heads, 2)),
            dma((2, nr, heads, 2)),
            dma((nf, heads, 2)),
            dma((nf, heads, 2)),
            dma((bits,)),
            dma((bits,)),
            dma((bits,)),
            dma((bits,)),
            dma((bits,)),
            dma((bits,)),
            dma((peers,)),
            dma((peers,)),
        ],
        compiler_params=pltpu.CompilerParams(
            collective_id=1, has_side_effects=True, vmem_limit_bytes=48 * 1024 * 1024
        ),
    )(
        attn,
        partials,
        text_key_grad,
        text_value_grad,
        pieces,
        grad_out,
        cosine,
        sine,
    )
    return (
        grad_query,
        grad_key,
        grad_value,
        text_key_sum,
        text_value_sum,
        grad_gate.reshape(-1),
    )


def solution(mesh):
    placed = (
        P("seq", "head"),
        P("seq", "head"),
        P("seq", "head"),
        P(None, "head"),
        P(None, "head"),
        P(),
        P("head", None),
        P(),
        P("head", None),
        P(),
        P("seq", "head"),
    )
    return jax.shard_map(
        on_device,
        mesh=mesh,
        in_specs=placed,
        out_specs=(
            P("seq", "head"),
            P("seq", "head"),
            P("seq", "head"),
            P(None, "head"),
            P(None, "head"),
            P(),
        ),
        check_vma=False,
    )
```

```python
import functools

import jax
import jax.numpy as jnp
import numpy as np
from jax import lax
from jax.experimental import pallas as pl
from jax.experimental.pallas import tpu as pltpu
from jax.sharding import PartitionSpec as P

HEAD_DIM = 128
TILE_T = 6
TILE_H = 8
TILE_W = 8
COLS = 8
THETA = 256.0
NEG = -1e30
F32 = jnp.float32
BF16 = jnp.bfloat16
MESH = pl.DeviceIdType.MESH


def lane_tables():
    first = HEAD_DIM // 8
    second = (HEAD_DIM - first) // 2
    freqs = np.zeros((HEAD_DIM,), np.float32)
    section = np.zeros((HEAD_DIM,), np.float32)
    sign = np.zeros((HEAD_DIM,), np.float32)
    offset = 0
    for number, length in enumerate((first, second, second)):
        half = length // 2
        f = (THETA ** (-2.0 * np.arange(half) / length)).astype(np.float32)
        freqs[offset : offset + half] = f
        freqs[offset + half : offset + length] = f
        section[offset : offset + length] = number
        sign[offset : offset + half] = -1.0
        sign[offset + half : offset + length] = 1.0
        offset += length
    return np.stack([freqs, section, sign] + [np.zeros_like(freqs)] * 5)


def partner(x):
    first = HEAD_DIM // 8
    second = (HEAD_DIM - first) // 2
    lane = lax.broadcasted_iota(jnp.int32, x.shape, 1)
    a = first // 2
    b = second // 2
    up_a = pltpu.roll(x, HEAD_DIM - a, 1)
    down_a = pltpu.roll(x, a, 1)
    up_b = pltpu.roll(x, HEAD_DIM - b, 1)
    down_b = pltpu.roll(x, b, 1)
    in_a = jnp.where(lane < a, up_a, down_a)
    is_first = (lane < first + b) | ((lane >= first + second) & (lane < first + second + b))
    in_b = jnp.where(is_first, up_b, down_b)
    return jnp.where(lane < first, in_a, in_b)


def neighbour(row, col, dr, dc, row_count):
    to_r, to_c = row + dr, col + dc
    ok = (to_c >= 0) & (to_c < COLS)
    if row_count == 2:
        to_r = (to_r + 2) % 2
    else:
        ok = ok & (to_r >= 0) & (to_r < row_count)
    return to_r * COLS + to_c, ok


def greet(axis_devices):
    barrier = pltpu.get_barrier_semaphore()
    for target, ok in axis_devices:
        if ok is None:
            pl.semaphore_signal(barrier, inc=1, device_id=target, device_id_type=MESH)
        else:

            @pl.when(ok)
            def _():
                pl.semaphore_signal(barrier, inc=1, device_id=target, device_id_type=MESH)

    count = 0
    for _, ok in axis_devices:
        count = count + (1 if ok is None else ok.astype(jnp.int32))
    pl.semaphore_wait(barrier, count)


def guarded(ok, act):
    if ok is None:
        act()
    else:
        pl.when(ok)(act)


def mega_kernel(row_deltas, row_count, seq_count, head_count, names, *refs):
    r = dict(zip(names, refs))
    kv_ref, qr_ref, ga_ref, wall_ref = r["kv"], r["qr"], r["ga"], r["wall"]
    part_ref, attn_ref = r["part"], r["attn"]
    s_ref, m_ref, l_ref, o_ref, dqa_ref = r["s"], r["m"], r["l"], r["o"], r["dqa"]
    acc = r["acc"]
    heads = kv_ref.shape[0]
    tile, width = qr_ref.shape
    text = r["tk"].shape[0]
    half = width // 2
    my_cols = wall_ref.shape[2]
    scale = HEAD_DIM ** (-0.5)
    device = lax.axis_index("seq")
    mine = lax.axis_index("head")
    row = device // COLS
    col = device % COLS
    core = device % 2
    bits = seq_count.bit_length() - 1
    seg = 2 * text // seq_count
    per = text // seg
    far_rows = [dr for dr in row_deltas if dr != 0]
    deltas = [(dr, dc) for dr in row_deltas for dc in (0, -1, 1)]
    nb = len(deltas)

    def seq_id(index):
        return (index, mine)

    def head_id(index):
        return (device, index)

    def part_of(h):
        return slice(h * HEAD_DIM, (h + 1) * HEAD_DIM)

    col_to = {dc: neighbour(row, col, 0, dc, row_count if row_count == 2 else 1 << 20) for dc in (-1, 1)}
    row_to = {}
    for dr in far_rows:
        index, ok = neighbour(row, col, dr, 0, row_count)
        row_to[dr] = (index, None if row_count == 2 else ok)
    opposite = {dr: (dr if row_count == 2 else -dr) for dr in far_rows}
    peers = [(mine + step) % head_count for step in range(1, head_count)]
    partner_at = []
    bit_at = []
    for b in range(bits):
        bit = (device // (1 << b)) % 2
        bit_at.append(bit)
        partner_at.append(device + (1 - 2 * bit) * (1 << b))
    sibling = partner_at[0]

    loads = {}
    own_at = pl.ds(pl.multiple_of(mine * my_cols, 128), my_cols)
    wanted = [
        ("k", r["k_hbm"], r["k"]),
        ("lanes", r["lanes_hbm"], r["lanes"]),
        ("q", r["q_hbm"], r["q"]),
        ("v", r["v_hbm"], r["v"]),
        ("grad", r["grad_hbm"], r["grad"]),
        ("gate", r["gate_hbm"].at[:, own_at], r["gate"]),
        ("w", r["w_hbm"].at[:, own_at], wall_ref.at[0]),
        ("tk", r["tk_hbm"], r["tk"]),
        ("tv", r["tv_hbm"], r["tv"]),
        ("mask", r["mask_hbm"], r["mask"]),
    ]
    for i, (name, src, dst) in enumerate(wanted):
        loads[name] = pltpu.make_async_copy(src, dst, r["load_s"].at[i])
        loads[name].start()

    friends = [(seq_id(col_to[dc][0]), col_to[dc][1]) for dc in (-1, 1)]
    friends += [(seq_id(row_to[dr][0]), row_to[dr][1]) for dr in far_rows]
    friends += [(seq_id(p), None) for p in partner_at]
    friends += [(head_id(p), None) for p in peers]
    greet(friends)

    sent = []

    def start(src, dst, ss, rs, target, ok=None):
        copy = pltpu.make_async_remote_copy(
            src_ref=src, dst_ref=dst, send_sem=ss, recv_sem=rs, device_id=target, device_id_type=MESH
        )
        guarded(ok, copy.start)
        sent.append((copy, ok))
        return copy

    row_copies = {}
    col_copies = {}

    def send_rows(src, h, k):
        for dr in far_rows:
            slot = row_deltas.index(opposite[dr])
            target, ok = row_to[dr]
            row_copies[slot, h, k] = start(
                src, kv_ref.at[h, slot * 3, k], r["row_ss"].at[slot - 1, h, k],
                r["row_rs"].at[slot - 1, h, k], seq_id(target), ok,
            )

    def send_cols(src, ri, h, k, have):
        for side, dc in ((0, -1), (1, 1)):
            target, ok = col_to[dc]
            number = ri * 3 + (2 if dc == -1 else 1)
            if have is not None:
                ok = ok & have
            col_copies[side, ri, h, k] = start(
                src, kv_ref.at[h, number, k], r["col_ss"].at[side, ri, h, k],
                r["col_rs"].at[side, ri, h, k], seq_id(target), ok,
            )

    rows_at = pl.ds(pl.multiple_of(core * half, half), half)
    w_copies = []

    def send_values(h):
        send_rows(r["v_hbm"].at[:, part_of(h)], h, 1)
        if h == 0:
            for step in range(1, head_count):
                cols_at = pl.ds(pl.multiple_of(peers[step - 1] * my_cols, 128), my_cols)
                w_copies.append(
                    start(
                        r["w_hbm"].at[rows_at, cols_at], wall_ref.at[step, rows_at, :],
                        r["w_ss"].at[step - 1], r["w_rs"].at[step - 1], head_id(peers[step - 1]),
                    )
                )
        send_cols(r["v_hbm"].at[:, part_of(h)], 0, h, 1, None)

    send_values(0)
    loads["lanes"].wait()
    freqs = r["lanes"][0:1, :]
    section = r["lanes"][1:2, :]
    sign = r["lanes"][2:3, :]
    cos_ref, sin_ref = r["cos"], r["sin"]

    def table(count, base):
        step = lax.broadcasted_iota(jnp.int32, (8, HEAD_DIM), 0)
        pos = (base * count + step).astype(F32)
        angle = pos * freqs
        return jnp.cos(angle), jnp.sin(angle) * sign

    cf, sf = table(TILE_T, r["tile"][device, 0])
    cr, sr = table(TILE_H, r["tile"][device, 1])
    cc, sc = table(TILE_W, r["tile"][device, 2])
    for t in range(TILE_T):
        for y in range(TILE_H):
            at = pl.ds((t * TILE_H + y) * TILE_W, TILE_W)
            for out, f, w, c in ((cos_ref, cf, cr, cc), (sin_ref, sf, sr, sc)):
                low = jnp.where(section == 0.0, f[t : t + 1, :], w[y : y + 1, :])
                full = jnp.broadcast_to(section, c.shape)
                out[at, :] = jnp.where(full < 2.0, jnp.broadcast_to(low, c.shape), c)
    loads["k"].wait()
    for h in range(heads):
        x = r["k"][:, part_of(h)].astype(F32)
        kv_ref[h, 0, 0] = (x * cos_ref[...] + partner(x) * sin_ref[...]).astype(BF16)
        if h > 0:
            send_values(h)
        send_rows(kv_ref.at[h, 0, 0], h, 0)
        send_cols(kv_ref.at[h, 0, 0], 0, h, 0, None)
    loads["q"].wait()
    loads["v"].wait()
    for h in range(heads):
        x = r["q"][:, part_of(h)].astype(F32)
        qr_ref[:, part_of(h)] = (x * cos_ref[...] + partner(x) * sin_ref[...]).astype(BF16)
        kv_ref[h, 0, 1] = r["v"][:, part_of(h)]

    for name in ("grad", "gate", "w", "tk", "tv", "mask"):
        loads[name].wait()
    grad_ref, proj = r["grad"], r["proj"]
    proj[...] = (grad_ref[...].astype(F32) * r["gate"][...]).astype(BF16)

    def times(step):
        return lax.dot_general(
            proj[...], wall_ref[step], (((1,), (1,)), ((), ())), preferred_element_type=F32
        )

    r["ga32"][...] = times(0)

    def forward(h, k):
        for dr in far_rows:
            slot = row_deltas.index(dr)
            have = row_to[dr][1]
            guarded(have, row_copies[slot, h, k].wait_recv)
            send_cols(kv_ref.at[h, slot * 3, k], slot, h, k, have)

    def arrive(ri, h, k):
        for side in (0, 1):
            came = col_to[1 if side == 0 else -1][1]
            if ri > 0 and row_to[row_deltas[ri]][1] is not None:
                came = came & row_to[row_deltas[ri]][1]
            guarded(came, col_copies[side, ri, h, k].wait_recv)

    def nt(a, b):
        return lax.dot_general(a, b, (((1,), (1,)), ((), ())), preferred_element_type=F32)

    def tn(a, b):
        return lax.dot_general(a, b, (((0,), (0,)), ((), ())), preferred_element_type=F32)

    def nn(a, b):
        return lax.dot_general(a, b, (((1,), (0,)), ((), ())), preferred_element_type=F32)

    text_at = slice(nb * tile, nb * tile + text)

    def at_of(number):
        return slice(number * tile, (number + 1) * tile)

    def there(number):
        dr, dc = deltas[number]
        ok = None
        if dc != 0:
            ok = col_to[dc][1]
        if dr != 0 and row_to[dr][1] is not None:
            ok = row_to[dr][1] if ok is None else ok & row_to[dr][1]
        return ok

    def score(h, number):
        def act():
            dr, dc = deltas[number]
            s = nt(kv_ref[h, number, 0], qr_ref[:, part_of(h)]) * scale
            if (dr, dc) != (0, 0):
                gap = jnp.maximum(
                    abs(dr) - r["reach"][h, 0], abs(dc) - r["reach"][h, 1]
                )
                s = jnp.where(jnp.full((1, tile), gap, jnp.int32) <= 0, s, NEG)
            s_ref[at_of(number), :] = s
            m_ref[...] = jnp.maximum(m_ref[...], jnp.max(s, axis=0, keepdims=True))

        guarded(there(number), act)

    def near_scores(h):
        s = nt(r["tk"][:, part_of(h)], qr_ref[:, part_of(h)]) * scale
        mask = jnp.broadcast_to(r["mask"][...].astype(F32), (8, text)).T[:, 0:1]
        s = jnp.where(mask == 1.0, s, NEG)
        s_ref[text_at, :] = s
        m_ref[...] = jnp.max(s, axis=0, keepdims=True)
        score(h, 0)
        arrive(0, h, 0)
        score(h, 1)
        score(h, 2)

    def far_scores(h):
        for ri in range(1, len(row_deltas)):
            score(h, ri * 3)
        for ri in range(1, len(row_deltas)):
            arrive(ri, h, 0)
            score(h, ri * 3 + 1)
            score(h, ri * 3 + 2)

    def soften(h):
        e = jnp.exp(s_ref[text_at, :] - m_ref[...])
        s_ref[text_at, :] = e
        l_ref[...] = jnp.sum(e, axis=0, keepdims=True)
        for number in range(nb):

            def act():
                e = jnp.exp(s_ref[at_of(number), :] - m_ref[...])
                s_ref[at_of(number), :] = e
                l_ref[...] += jnp.sum(e, axis=0, keepdims=True)

            guarded(there(number), act)
        l_ref[...] = 1.0 / l_ref[...]

    def outputs(h):
        g = ga_ref[:, part_of(h)]
        p = (s_ref[text_at, :] * l_ref[...]).astype(BF16)
        o_ref[...] = tn(r["tv"][:, part_of(h)], p)
        dtv = nn(p, g)
        for i in range(per):
            acc[per + i, :, part_of(h)] = dtv[i * seg : (i + 1) * seg, :]
        for number in range(nb):
            if number % 3 == 1:
                arrive(number // 3, h, 1)

            def act():
                p = (s_ref[at_of(number), :] * l_ref[...]).astype(BF16)
                o_ref[...] += tn(kv_ref[h, number, 1], p)
                part_ref[h, number, 1] = nn(p, g).astype(BF16)

            guarded(there(number), act)
        attn = o_ref[...].T.astype(BF16)
        attn_ref[h] = attn
        product = g.astype(F32) * attn.astype(F32)
        m_ref[...] = jnp.sum(product.T, axis=0, keepdims=True)

    def grads(h, hooks):
        g = ga_ref[:, part_of(h)]
        q = qr_ref[:, part_of(h)]
        ds = s_ref[text_at, :] * l_ref[...] * (nt(r["tv"][:, part_of(h)], g) - m_ref[...])
        ds = ds.astype(BF16)
        dqa_ref[...] = tn(r["tk"][:, part_of(h)], ds)
        dtk = nn(ds, q) * scale
        for i in range(per):
            acc[i, :, part_of(h)] = dtk[i * seg : (i + 1) * seg, :]
        order = [n for n in range(nb) if n >= 3] + list(range(min(nb, 3)))
        for place, number in enumerate(order):
            if place % 2 == 0 and hooks:
                hooks.pop(0)()

            def act():
                dp = nt(kv_ref[h, number, 1], g)
                ds = (s_ref[at_of(number), :] * l_ref[...] * (dp - m_ref[...])).astype(BF16)
                dqa_ref[...] += tn(kv_ref[h, number, 0], ds)
                part_ref[h, number, 0] = (nn(ds, q) * scale).astype(BF16)

            guarded(there(number), act)
            if number % 3 == 2:
                return_cols(number // 3, h)
        while hooks:
            hooks.pop(0)()
        dq = dqa_ref[...].T * scale
        r["dq"][:, part_of(h)] = (dq * cos_ref[...] - partner(dq) * sin_ref[...]).astype(BF16)

    back_cols = {}

    def return_cols(ri, h):
        for k in (1, 0):
            for side, dc in ((0, -1), (1, 1)):
                target, ok = col_to[dc]
                have = row_to[row_deltas[ri]][1] if ri > 0 else None
                if have is not None:
                    ok = ok & have
                back_cols[ri, h, k, side] = start(
                    part_ref.at[h, ri * 3 + 1 + side, k], r["bcol_in"].at[side, ri, h, k],
                    r["bcol_ss"].at[side, ri, h, k], r["bcol_rs"].at[side, ri, h, k],
                    seq_id(target), ok,
                )

    def col_sum(ri, h, k):
        total = part_ref[h, ri * 3, k].astype(F32)
        have = row_to[row_deltas[ri]][1] if ri > 0 else None
        for side, dc in ((0, -1), (1, 1)):
            came = col_to[-dc][1]
            waits = came if have is None else came & have
            guarded(waits, back_cols[ri, h, k, side].wait_recv)
            got = r["bcol_in"][side, ri, h, k].astype(F32)
            total = total + jnp.where(came, got, 0.0)
        return total

    back_rows = {}

    def return_rows(h, k):
        for fi, dr in enumerate(far_rows):
            target, ok = row_to[dr]

            def act():
                r["brow_out"][fi, h, k] = col_sum(fi + 1, h, k).astype(BF16)

            guarded(ok, act)
            back_rows[fi, h, k] = start(
                r["brow_out"].at[fi, h, k], r["brow_in"].at[fi, h, k],
                r["brow_ss"].at[fi, h, k], r["brow_rs"].at[fi, h, k], seq_id(target), ok,
            )

    attn_copies = []

    def send_attn(h):
        for step in range(1, head_count):
            attn_copies.append(
                start(
                    attn_ref.at[h], r["attn_in"].at[step - 1, h],
                    r["attn_ss"].at[step - 1, h], r["attn_rs"].at[step - 1, h],
                    head_id(peers[step - 1]),
                )
            )

    starts = [0]
    state = []

    def halve(b):
        n = seq_count >> (b + 1)
        keep = starts[-1] + bit_at[b] * n
        give = starts[-1] + (1 - bit_at[b]) * n
        r["text_out"][pl.ds(n, n)] = acc[pl.ds(give, n)].astype(BF16)
        copy = start(
            r["text_out"].at[pl.ds(n, n)], r["text_in"].at[pl.ds(n, n)],
            r["text_ss"].at[b], r["text_rs"].at[b], seq_id(partner_at[b]),
        )
        starts.append(keep)
        state.append((copy, keep, n))

    def finish():
        copy, keep, n = state[-1]
        copy.wait_recv()
        acc[pl.ds(keep, n)] = acc[pl.ds(keep, n)] + r["text_in"][pl.ds(n, n)].astype(F32)

    def text_stage(b):
        def act():
            if b > 0:
                finish()
            halve(b)

        return act

    forward(0, 1)
    near_scores(0)
    swaps = []
    for step in range(1, head_count):
        w_copies[step - 1].wait_recv()
        swaps.append(
            start(
                wall_ref.at[step, rows_at, :], wall_ref.at[step, rows_at, :],
                r["swap_ss"].at[step - 1], r["swap_rs"].at[step - 1], seq_id(sibling),
            )
        )
    forward(0, 0)
    parts = []
    for step in range(1, head_count):
        swaps[step - 1].wait_recv()
        r["part_out"][step - 1] = times(step).astype(BF16)
        back = (mine + head_count - step) % head_count
        parts.append(
            start(
                r["part_out"].at[step - 1], r["part_in"].at[step - 1],
                r["part_ss"].at[step - 1], r["part_rs"].at[step - 1], head_id(back),
            )
        )
    far_scores(0)
    for h in range(1, heads):
        forward(h, 1)
    soften(0)
    total = r["ga32"][...]
    for step in range(1, head_count):
        parts[step - 1].wait_recv()
        total = total + r["part_in"][step - 1].astype(F32)
    ga_ref[...] = total.astype(BF16)
    outputs(0)
    send_attn(0)
    for h in range(1, heads):
        forward(h, 0)
    grads(0, [text_stage(b) for b in range(bits)] if heads == 1 else [])
    for h in range(1, heads):
        near_scores(h)
        return_rows(h - 1, 1)
        far_scores(h)
        return_rows(h - 1, 0)
        soften(h)
        outputs(h)
        send_attn(h)
        grads(h, [text_stage(b) for b in range(bits)] if h == heads - 1 else [])

    finish()
    base = starts[-1]
    text_res = r["text_res"]
    text_res[pl.ds(base, 1)] = acc[pl.ds(base, 1)].astype(BF16)

    def gather(b):
        n = seq_count >> (b + 1)
        at = starts[b + 1]
        return start(
            text_res.at[pl.ds(at, n)], text_res.at[pl.ds(at, n)],
            r["gather_ss"].at[b], r["gather_rs"].at[b], seq_id(partner_at[b]),
        )

    gathering = gather(bits - 1)
    return_rows(heads - 1, 1)
    return_rows(heads - 1, 0)

    for copy in attn_copies:
        copy.wait_recv()
    gate_acc = r["gate_acc"]
    piece = 384 if my_cols % 384 == 0 else 128
    for c in range(my_cols // piece):
        at = slice(c * piece, (c + 1) * piece)
        total = jnp.zeros((tile, piece), F32)
        for step in range(head_count):
            for h in range(heads):
                left = attn_ref[h] if step == 0 else r["attn_in"][step - 1, h]
                total = total + jnp.dot(
                    left, wall_ref[step, part_of(h), at], preferred_element_type=F32
                )
        gate_acc[:, at] = jnp.sum(grad_ref[:, at].astype(F32) * total, axis=0, keepdims=True)
    for b in range(bits):
        r["gate_out"][b] = gate_acc[...]
        copy = start(
            r["gate_out"].at[b], r["gate_in"].at[b], r["gate_ss"].at[b], r["gate_rs"].at[b],
            seq_id(partner_at[b]),
        )
        back_bit = bits - 1 - b
        gathering.wait_recv()
        if back_bit > 0:
            gathering = gather(back_bit - 1)
        copy.wait_recv()
        gate_acc[...] = gate_acc[...] + r["gate_in"][b]
    gate_all = r["gate_all"]
    gate_all[mine] = gate_acc[...]
    all_copies = []
    for step in range(1, head_count):
        all_copies.append(
            start(
                gate_acc, gate_all.at[mine], r["all_ss"].at[step - 1], r["all_rs"].at[step - 1],
                head_id(peers[step - 1]),
            )
        )
    for i in range(per):
        r["dtk"][i * seg : (i + 1) * seg, :] = text_res[i]
        r["dtv"][i * seg : (i + 1) * seg, :] = text_res[per + i]

    for h in range(heads):
        for k in (1, 0):
            total = col_sum(0, h, k)
            for fi, dr in enumerate(far_rows):
                came = row_to[opposite[dr]][1]
                guarded(came, back_rows[fi, h, k].wait_recv)
                got = r["brow_in"][fi, h, k].astype(F32)
                total = total + (got if came is None else jnp.where(came, got, 0.0))
            if k == 0:
                r["dk"][:, part_of(h)] = (
                    total * cos_ref[...] - partner(total) * sin_ref[...]
                ).astype(BF16)
            else:
                r["dv"][:, part_of(h)] = total.astype(BF16)
    for copy in all_copies:
        copy.wait_recv()
    for i in range(head_count):
        r["dgate"][:, i * my_cols : (i + 1) * my_cols] = gate_all[i]
    for copy, ok in sent:
        guarded(ok, copy.wait_send)


def on_device(
    query_in,
    key_in,
    value_in,
    text_keys,
    text_values,
    text_mask,
    window_reach,
    tile_map,
    out_weight,
    gate_scale,
    grad_out,
):
    tile, width = query_in.shape
    heads = width // HEAD_DIM
    text = text_keys.shape[0]
    seq_count = lax.axis_size("seq")
    head_count = lax.axis_size("head")
    row_count = seq_count // COLS
    my_cols = grad_out.shape[1]
    row_deltas = (0,) if row_count == 1 else (0, 1) if row_count == 2 else (0, -1, 1)
    nr = len(row_deltas)
    nb = 3 * nr
    nf = max(nr - 1, 1)
    peers = max(head_count - 1, 1)
    bits = seq_count.bit_length() - 1
    seg = 2 * text // seq_count
    dma = pltpu.SemaphoreType.DMA
    vmem = pl.BlockSpec(memory_space=pltpu.VMEM)
    smem = pl.BlockSpec(memory_space=pltpu.SMEM)
    hbm = pl.BlockSpec(memory_space=pl.ANY)
    lanes = lane_tables()
    inputs = [
        ("tile", tile_map, smem),
        ("reach", window_reach, smem),
        ("lanes_hbm", jnp.asarray(lanes), hbm),
        ("q_hbm", query_in, hbm),
        ("k_hbm", key_in, hbm),
        ("v_hbm", value_in, hbm),
        ("tk_hbm", text_keys, hbm),
        ("tv_hbm", text_values, hbm),
        ("mask_hbm", text_mask[None, :], hbm),
        ("w_hbm", out_weight, hbm),
        ("gate_hbm", gate_scale[None, :], hbm),
        ("grad_hbm", grad_out, hbm),
    ]
    outputs = [
        ("dq", (tile, width), BF16),
        ("dk", (tile, width), BF16),
        ("dv", (tile, width), BF16),
        ("dtk", (text, width), BF16),
        ("dtv", (text, width), BF16),
        ("dgate", (1, head_count * my_cols), F32),
    ]
    buffers = [
        ("lanes", lanes.shape, F32),
        ("q", (tile, width), BF16),
        ("k", (tile, width), BF16),
        ("v", (tile, width), BF16),
        ("tk", (text, width), BF16),
        ("tv", (text, width), BF16),
        ("mask", (1, text), jnp.int32),
        ("gate", (1, my_cols), F32),
        ("grad", (tile, my_cols), BF16),
        ("qr", (tile, width), BF16),
        ("kv", (heads, nb, 2, tile, HEAD_DIM), BF16),
        ("part", (heads, nb, 2, tile, HEAD_DIM), BF16),
        ("cos", (tile, HEAD_DIM), F32),
        ("sin", (tile, HEAD_DIM), F32),
        ("wall", (head_count, width, my_cols), BF16),
        ("ga", (tile, width), BF16),
        ("ga32", (tile, width), F32),
        ("proj", (tile, my_cols), BF16),
        ("part_out", (peers, tile, width), BF16),
        ("part_in", (peers, tile, width), BF16),
        ("attn", (heads, tile, HEAD_DIM), BF16),
        ("attn_in", (peers, heads, tile, HEAD_DIM), BF16),
        ("s", (nb * tile + text, tile), F32),
        ("m", (1, tile), F32),
        ("l", (1, tile), F32),
        ("o", (HEAD_DIM, tile), F32),
        ("dqa", (HEAD_DIM, tile), F32),
        ("bcol_in", (2, nr, heads, 2, tile, HEAD_DIM), BF16),
        ("brow_out", (nf, heads, 2, tile, HEAD_DIM), BF16),
        ("brow_in", (nf, heads, 2, tile, HEAD_DIM), BF16),
        ("acc", (seq_count, seg, width), F32),
        ("text_out", (seq_count, seg, width), BF16),
        ("text_in", (seq_count, seg, width), BF16),
        ("text_res", (seq_count, seg, width), BF16),
        ("gate_acc", (1, my_cols), F32),
        ("gate_out", (bits, 1, my_cols), F32),
        ("gate_in", (bits, 1, my_cols), F32),
        ("gate_all", (head_count, 1, my_cols), F32),
    ]
    semaphores = [("load_s", (10,))]
    for name, shape in (
        ("row", (nf, heads, 2)),
        ("col", (2, nr, heads, 2)),
        ("w", (peers,)),
        ("swap", (peers,)),
        ("part", (peers,)),
        ("attn", (peers, heads)),
        ("bcol", (2, nr, heads, 2)),
        ("brow", (nf, heads, 2)),
        ("text", (bits,)),
        ("gather", (bits,)),
        ("gate", (bits,)),
        ("all", (peers,)),
    ):
        semaphores += [(name + "_ss", shape), (name + "_rs", shape)]
    names = [entry[0] for entry in inputs + outputs + buffers + semaphores]
    results = pl.pallas_call(
        functools.partial(mega_kernel, row_deltas, row_count, seq_count, head_count, names),
        out_shape=[jax.ShapeDtypeStruct(shape, kind) for _, shape, kind in outputs],
        in_specs=[spec for _, _, spec in inputs],
        out_specs=[vmem] * len(outputs),
        scratch_shapes=[pltpu.VMEM(shape, kind) for _, shape, kind in buffers]
        + [dma(shape) for _, shape in semaphores],
        compiler_params=pltpu.CompilerParams(
            collective_id=0, has_side_effects=True, vmem_limit_bytes=60 * 1024 * 1024
        ),
    )(*[array for _, array, _ in inputs])
    return (*results[:5], results[5].reshape(-1))


def solution(mesh):
    placed = (
        P("seq", "head"),
        P("seq", "head"),
        P("seq", "head"),
        P(None, "head"),
        P(None, "head"),
        P(),
        P("head", None),
        P(),
        P("head", None),
        P(),
        P("seq", "head"),
    )
    return jax.shard_map(
        on_device,
        mesh=mesh,
        in_specs=placed,
        out_specs=(
            P("seq", "head"),
            P("seq", "head"),
            P("seq", "head"),
            P(None, "head"),
            P(None, "head"),
            P(),
        ),
        check_vma=False,
    )
```

```python
import functools

import jax
import jax.numpy as jnp
import numpy as np
from jax import lax
from jax.experimental import pallas as pl
from jax.experimental.pallas import tpu as pltpu
from jax.sharding import PartitionSpec as P

HEAD_DIM = 128
TILE_T = 6
TILE_H = 8
TILE_W = 8
COLS = 8
THETA = 256.0
NEG = -1e30
F32 = jnp.float32
BF16 = jnp.bfloat16
MESH = pl.DeviceIdType.MESH


def lane_tables():
    first = HEAD_DIM // 8
    second = (HEAD_DIM - first) // 2
    freqs = np.zeros((HEAD_DIM,), np.float32)
    section = np.zeros((HEAD_DIM,), np.float32)
    sign = np.zeros((HEAD_DIM,), np.float32)
    offset = 0
    for number, length in enumerate((first, second, second)):
        half = length // 2
        f = (THETA ** (-2.0 * np.arange(half) / length)).astype(np.float32)
        freqs[offset : offset + half] = f
        freqs[offset + half : offset + length] = f
        section[offset : offset + length] = number
        sign[offset : offset + half] = -1.0
        sign[offset + half : offset + length] = 1.0
        offset += length
    return np.stack([freqs, section, sign] + [np.zeros_like(freqs)] * 5)


def partner(x):
    first = HEAD_DIM // 8
    second = (HEAD_DIM - first) // 2
    lane = lax.broadcasted_iota(jnp.int32, x.shape, 1)
    a = first // 2
    b = second // 2
    up_a = pltpu.roll(x, HEAD_DIM - a, 1)
    down_a = pltpu.roll(x, a, 1)
    up_b = pltpu.roll(x, HEAD_DIM - b, 1)
    down_b = pltpu.roll(x, b, 1)
    in_a = jnp.where(lane < a, up_a, down_a)
    is_first = (lane < first + b) | ((lane >= first + second) & (lane < first + second + b))
    in_b = jnp.where(is_first, up_b, down_b)
    return jnp.where(lane < first, in_a, in_b)


def neighbour(row, col, dr, dc, row_count):
    to_r, to_c = row + dr, col + dc
    ok = (to_c >= 0) & (to_c < COLS)
    if row_count == 2:
        to_r = (to_r + 2) % 2
    else:
        ok = ok & (to_r >= 0) & (to_r < row_count)
    return to_r * COLS + to_c, ok


def greet(axis_devices):
    barrier = pltpu.get_barrier_semaphore()
    for target, ok in axis_devices:
        if ok is None:
            pl.semaphore_signal(barrier, inc=1, device_id=target, device_id_type=MESH)
        else:

            @pl.when(ok)
            def _():
                pl.semaphore_signal(barrier, inc=1, device_id=target, device_id_type=MESH)

    count = 0
    for _, ok in axis_devices:
        count = count + (1 if ok is None else ok.astype(jnp.int32))
    pl.semaphore_wait(barrier, count)


def guarded(ok, act):
    if ok is None:
        act()
    else:
        pl.when(ok)(act)


def mega_kernel(row_deltas, row_count, seq_count, head_count, names, *refs):
    r = dict(zip(names, refs))
    kv_ref, qr_ref, ga_ref, wall_ref = r["kv"], r["qr"], r["ga"], r["wall"]
    part_ref, attn_ref = r["part"], r["attn"]
    s_ref, m_ref, l_ref, o_ref, dqa_ref = r["s"], r["m"], r["l"], r["o"], r["dqa"]
    acc = r["acc"]
    heads = kv_ref.shape[0]
    tile, width = qr_ref.shape
    text = r["tk"].shape[0]
    half = width // 2
    my_cols = wall_ref.shape[2]
    scale = HEAD_DIM ** (-0.5)
    device = lax.axis_index("seq")
    mine = lax.axis_index("head")
    row = device // COLS
    col = device % COLS
    core = device % 2
    bits = seq_count.bit_length() - 1
    seg = 2 * text // seq_count
    per = text // seg
    far_rows = [dr for dr in row_deltas if dr != 0]
    deltas = [(dr, dc) for dr in row_deltas for dc in (0, -1, 1)]
    nb = len(deltas)

    def seq_id(index):
        return (index, mine)

    def head_id(index):
        return (device, index)

    def part_of(h):
        return slice(h * HEAD_DIM, (h + 1) * HEAD_DIM)

    col_to = {dc: neighbour(row, col, 0, dc, row_count if row_count == 2 else 1 << 20) for dc in (-1, 1)}
    row_to = {}
    for dr in far_rows:
        index, ok = neighbour(row, col, dr, 0, row_count)
        row_to[dr] = (index, None if row_count == 2 else ok)
    opposite = {dr: (dr if row_count == 2 else -dr) for dr in far_rows}
    peers = [(mine + step) % head_count for step in range(1, head_count)]
    partner_at = []
    bit_at = []
    for b in range(bits):
        bit = (device // (1 << b)) % 2
        bit_at.append(bit)
        partner_at.append(device + (1 - 2 * bit) * (1 << b))
    sibling = partner_at[0]

    loads = {}
    own_at = pl.ds(pl.multiple_of(mine * my_cols, 128), my_cols)
    wanted = [
        ("k", r["k_hbm"], r["k"]),
        ("lanes", r["lanes_hbm"], r["lanes"]),
        ("q", r["q_hbm"], r["q"]),
        ("v", r["v_hbm"], r["v"]),
        ("grad", r["grad_hbm"], r["grad"]),
        ("gate", r["gate_hbm"].at[:, own_at], r["gate"]),
        ("w", r["w_hbm"].at[:, own_at], wall_ref.at[0]),
        ("tk", r["tk_hbm"], r["tk"]),
        ("tv", r["tv_hbm"], r["tv"]),
        ("mask", r["mask_hbm"], r["mask"]),
    ]
    for i, (name, src, dst) in enumerate(wanted):
        loads[name] = pltpu.make_async_copy(src, dst, r["load_s"].at[i])
        loads[name].start()

    friends = [(seq_id(col_to[dc][0]), col_to[dc][1]) for dc in (-1, 1)]
    friends += [(seq_id(row_to[dr][0]), row_to[dr][1]) for dr in far_rows]
    friends += [(seq_id(p), None) for p in partner_at]
    friends += [(head_id(p), None) for p in peers]
    greet(friends)

    sent = []

    def start(src, dst, ss, rs, target, ok=None):
        copy = pltpu.make_async_remote_copy(
            src_ref=src, dst_ref=dst, send_sem=ss, recv_sem=rs, device_id=target, device_id_type=MESH
        )
        guarded(ok, copy.start)
        sent.append((copy, ok))
        return copy

    row_copies = {}
    col_copies = {}

    def send_rows(src, h, k):
        for dr in far_rows:
            slot = row_deltas.index(opposite[dr])
            target, ok = row_to[dr]
            row_copies[slot, h, k] = start(
                src, kv_ref.at[h, slot * 3, k], r["row_ss"].at[slot - 1, h, k],
                r["row_rs"].at[slot - 1, h, k], seq_id(target), ok,
            )

    def send_cols(src, ri, h, k, have):
        for side, dc in ((0, -1), (1, 1)):
            target, ok = col_to[dc]
            number = ri * 3 + (2 if dc == -1 else 1)
            if have is not None:
                ok = ok & have
            col_copies[side, ri, h, k] = start(
                src, kv_ref.at[h, number, k], r["col_ss"].at[side, ri, h, k],
                r["col_rs"].at[side, ri, h, k], seq_id(target), ok,
            )

    rows_at = pl.ds(pl.multiple_of(core * half, half), half)
    w_copies = []

    def send_values(h):
        send_rows(r["v_hbm"].at[:, part_of(h)], h, 1)
        if h == 0:
            for step in range(1, head_count):
                cols_at = pl.ds(pl.multiple_of(peers[step - 1] * my_cols, 128), my_cols)
                w_copies.append(
                    start(
                        r["w_hbm"].at[rows_at, cols_at], wall_ref.at[step, rows_at, :],
                        r["w_ss"].at[step - 1], r["w_rs"].at[step - 1], head_id(peers[step - 1]),
                    )
                )
        send_cols(r["v_hbm"].at[:, part_of(h)], 0, h, 1, None)

    send_values(0)
    loads["lanes"].wait()
    freqs = r["lanes"][0:1, :]
    section = r["lanes"][1:2, :]
    sign = r["lanes"][2:3, :]
    cos_ref, sin_ref = r["cos"], r["sin"]

    def table(count, base):
        step = lax.broadcasted_iota(jnp.int32, (8, HEAD_DIM), 0)
        pos = (base * count + step).astype(F32)
        angle = pos * freqs
        return jnp.cos(angle), jnp.sin(angle) * sign

    cf, sf = table(TILE_T, r["tile"][device, 0])
    cr, sr = table(TILE_H, r["tile"][device, 1])
    cc, sc = table(TILE_W, r["tile"][device, 2])
    for t in range(TILE_T):
        for y in range(TILE_H):
            at = pl.ds((t * TILE_H + y) * TILE_W, TILE_W)
            for out, f, w, c in ((cos_ref, cf, cr, cc), (sin_ref, sf, sr, sc)):
                low = jnp.where(section == 0.0, f[t : t + 1, :], w[y : y + 1, :])
                full = jnp.broadcast_to(section, c.shape)
                out[at, :] = jnp.where(full < 2.0, jnp.broadcast_to(low, c.shape), c)
    loads["k"].wait()
    for h in range(heads):
        x = r["k"][:, part_of(h)].astype(F32)
        kv_ref[h, 0, 0] = (x * cos_ref[...] + partner(x) * sin_ref[...]).astype(BF16)
        if h > 0:
            send_values(h)
        send_rows(kv_ref.at[h, 0, 0], h, 0)
        send_cols(kv_ref.at[h, 0, 0], 0, h, 0, None)
    loads["q"].wait()
    loads["v"].wait()
    for h in range(heads):
        x = r["q"][:, part_of(h)].astype(F32)
        qr_ref[:, part_of(h)] = (x * cos_ref[...] + partner(x) * sin_ref[...]).astype(BF16)
        kv_ref[h, 0, 1] = r["v"][:, part_of(h)]

    for name in ("grad", "gate", "w", "tk", "tv", "mask"):
        loads[name].wait()
    grad_ref, proj = r["grad"], r["proj"]
    proj[...] = (grad_ref[...].astype(F32) * r["gate"][...]).astype(BF16)

    def times(step):
        return lax.dot_general(
            proj[...], wall_ref[step], (((1,), (1,)), ((), ())), preferred_element_type=F32
        )

    r["ga32"][...] = times(0)

    def forward(h, k):
        for dr in far_rows:
            slot = row_deltas.index(dr)
            have = row_to[dr][1]
            guarded(have, row_copies[slot, h, k].wait_recv)
            send_cols(kv_ref.at[h, slot * 3, k], slot, h, k, have)

    def arrive(ri, h, k):
        for side in (0, 1):
            came = col_to[1 if side == 0 else -1][1]
            if ri > 0 and row_to[row_deltas[ri]][1] is not None:
                came = came & row_to[row_deltas[ri]][1]
            guarded(came, col_copies[side, ri, h, k].wait_recv)

    def nt(a, b):
        return lax.dot_general(a, b, (((1,), (1,)), ((), ())), preferred_element_type=F32)

    def tn(a, b):
        return lax.dot_general(a, b, (((0,), (0,)), ((), ())), preferred_element_type=F32)

    def nn(a, b):
        return lax.dot_general(a, b, (((1,), (0,)), ((), ())), preferred_element_type=F32)

    text_at = slice(nb * tile, nb * tile + text)

    def at_of(number):
        return slice(number * tile, (number + 1) * tile)

    def there(number):
        dr, dc = deltas[number]
        ok = None
        if dc != 0:
            ok = col_to[dc][1]
        if dr != 0 and row_to[dr][1] is not None:
            ok = row_to[dr][1] if ok is None else ok & row_to[dr][1]
        return ok

    def score(h, number):
        def act():
            dr, dc = deltas[number]
            s = nt(kv_ref[h, number, 0], qr_ref[:, part_of(h)]) * scale
            if (dr, dc) != (0, 0):
                gap = jnp.maximum(
                    abs(dr) - r["reach"][h, 0], abs(dc) - r["reach"][h, 1]
                )
                s = jnp.where(jnp.full((1, tile), gap, jnp.int32) <= 0, s, NEG)
            s_ref[at_of(number), :] = s
            m_ref[...] = jnp.maximum(m_ref[...], jnp.max(s, axis=0, keepdims=True))

        guarded(there(number), act)

    def near_scores(h):
        s = nt(r["tk"][:, part_of(h)], qr_ref[:, part_of(h)]) * scale
        mask = jnp.broadcast_to(r["mask"][...].astype(F32), (8, text)).T[:, 0:1]
        s = jnp.where(mask == 1.0, s, NEG)
        s_ref[text_at, :] = s
        m_ref[...] = jnp.max(s, axis=0, keepdims=True)
        score(h, 0)
        arrive(0, h, 0)
        score(h, 1)
        score(h, 2)

    def far_scores(h):
        for ri in range(1, len(row_deltas)):
            score(h, ri * 3)
        for ri in range(1, len(row_deltas)):
            arrive(ri, h, 0)
            score(h, ri * 3 + 1)
            score(h, ri * 3 + 2)

    def soften(h):
        e = jnp.exp(s_ref[text_at, :] - m_ref[...])
        s_ref[text_at, :] = e
        l_ref[...] = jnp.sum(e, axis=0, keepdims=True)
        for number in range(nb):

            def act():
                e = jnp.exp(s_ref[at_of(number), :] - m_ref[...])
                s_ref[at_of(number), :] = e
                l_ref[...] += jnp.sum(e, axis=0, keepdims=True)

            guarded(there(number), act)
        l_ref[...] = 1.0 / l_ref[...]

    def outputs(h):
        g = ga_ref[:, part_of(h)]
        p = (s_ref[text_at, :] * l_ref[...]).astype(BF16)
        o_ref[...] = tn(r["tv"][:, part_of(h)], p)
        dtv = nn(p, g)
        for i in range(per):
            acc[per + i, :, part_of(h)] = dtv[i * seg : (i + 1) * seg, :]
        for number in range(nb):
            if number % 3 == 1:
                arrive(number // 3, h, 1)

            def act():
                p = (s_ref[at_of(number), :] * l_ref[...]).astype(BF16)
                o_ref[...] += tn(kv_ref[h, number, 1], p)
                part_ref[h, number, 1] = nn(p, g).astype(BF16)

            guarded(there(number), act)
        attn = o_ref[...].T.astype(BF16)
        attn_ref[h] = attn
        product = g.astype(F32) * attn.astype(F32)
        m_ref[...] = jnp.sum(product.T, axis=0, keepdims=True)

    def grads(h, hooks):
        g = ga_ref[:, part_of(h)]
        q = qr_ref[:, part_of(h)]
        ds = s_ref[text_at, :] * l_ref[...] * (nt(r["tv"][:, part_of(h)], g) - m_ref[...])
        ds = ds.astype(BF16)
        dqa_ref[...] = tn(r["tk"][:, part_of(h)], ds)
        dtk = nn(ds, q) * scale
        for i in range(per):
            acc[i, :, part_of(h)] = dtk[i * seg : (i + 1) * seg, :]
        order = [n for n in range(nb) if n >= 3] + list(range(min(nb, 3)))
        for place, number in enumerate(order):
            if place % 2 == 0 and hooks:
                hooks.pop(0)()

            def act():
                dp = nt(kv_ref[h, number, 1], g)
                ds = (s_ref[at_of(number), :] * l_ref[...] * (dp - m_ref[...])).astype(BF16)
                dqa_ref[...] += tn(kv_ref[h, number, 0], ds)
                part_ref[h, number, 0] = (nn(ds, q) * scale).astype(BF16)

            guarded(there(number), act)
            if number % 3 == 2:
                return_cols(number // 3, h)
        while hooks:
            hooks.pop(0)()
        dq = dqa_ref[...].T * scale
        r["dq"][:, part_of(h)] = (dq * cos_ref[...] - partner(dq) * sin_ref[...]).astype(BF16)

    back_cols = {}

    def return_cols(ri, h):
        for k in (1, 0):
            for side, dc in ((0, -1), (1, 1)):
                target, ok = col_to[dc]
                have = row_to[row_deltas[ri]][1] if ri > 0 else None
                if have is not None:
                    ok = ok & have
                back_cols[ri, h, k, side] = start(
                    part_ref.at[h, ri * 3 + 1 + side, k], r["bcol_in"].at[side, ri, h, k],
                    r["bcol_ss"].at[side, ri, h, k], r["bcol_rs"].at[side, ri, h, k],
                    seq_id(target), ok,
                )

    def col_sum(ri, h, k):
        total = part_ref[h, ri * 3, k].astype(F32)
        have = row_to[row_deltas[ri]][1] if ri > 0 else None
        for side, dc in ((0, -1), (1, 1)):
            came = col_to[-dc][1]
            waits = came if have is None else came & have
            guarded(waits, back_cols[ri, h, k, side].wait_recv)
            got = r["bcol_in"][side, ri, h, k].astype(F32)
            total = total + jnp.where(came, got, 0.0)
        return total

    back_rows = {}

    def return_rows(h, k):
        for fi, dr in enumerate(far_rows):
            target, ok = row_to[dr]

            def act():
                r["brow_out"][fi, h, k] = col_sum(fi + 1, h, k).astype(BF16)

            guarded(ok, act)
            back_rows[fi, h, k] = start(
                r["brow_out"].at[fi, h, k], r["brow_in"].at[fi, h, k],
                r["brow_ss"].at[fi, h, k], r["brow_rs"].at[fi, h, k], seq_id(target), ok,
            )

    attn_copies = []

    def send_attn(h):
        for step in range(1, head_count):
            attn_copies.append(
                start(
                    attn_ref.at[h], r["attn_in"].at[step - 1, h],
                    r["attn_ss"].at[step - 1, h], r["attn_rs"].at[step - 1, h],
                    head_id(peers[step - 1]),
                )
            )

    starts = [0]
    state = []

    def halve(b):
        n = seq_count >> (b + 1)
        keep = starts[-1] + bit_at[b] * n
        give = starts[-1] + (1 - bit_at[b]) * n
        r["text_out"][pl.ds(n, n)] = acc[pl.ds(give, n)].astype(BF16)
        copy = start(
            r["text_out"].at[pl.ds(n, n)], r["text_in"].at[pl.ds(n, n)],
            r["text_ss"].at[b], r["text_rs"].at[b], seq_id(partner_at[b]),
        )
        starts.append(keep)
        state.append((copy, keep, n))

    def finish():
        copy, keep, n = state[-1]
        copy.wait_recv()
        acc[pl.ds(keep, n)] = acc[pl.ds(keep, n)] + r["text_in"][pl.ds(n, n)].astype(F32)

    def text_stage(b):
        def act():
            if b > 0:
                finish()
            halve(b)

        return act

    forward(0, 1)
    near_scores(0)
    swaps = []
    for step in range(1, head_count):
        w_copies[step - 1].wait_recv()
        swaps.append(
            start(
                wall_ref.at[step, rows_at, :], wall_ref.at[step, rows_at, :],
                r["swap_ss"].at[step - 1], r["swap_rs"].at[step - 1], seq_id(sibling),
            )
        )
    forward(0, 0)
    parts = []
    for step in range(1, head_count):
        swaps[step - 1].wait_recv()
        r["part_out"][step - 1] = times(step).astype(BF16)
        back = (mine + head_count - step) % head_count
        parts.append(
            start(
                r["part_out"].at[step - 1], r["part_in"].at[step - 1],
                r["part_ss"].at[step - 1], r["part_rs"].at[step - 1], head_id(back),
            )
        )
    far_scores(0)
    for h in range(1, heads):
        forward(h, 1)
    soften(0)
    total = r["ga32"][...]
    for step in range(1, head_count):
        parts[step - 1].wait_recv()
        total = total + r["part_in"][step - 1].astype(F32)
    ga_ref[...] = total.astype(BF16)
    outputs(0)
    send_attn(0)
    for h in range(1, heads):
        forward(h, 0)
    grads(0, [text_stage(b) for b in range(bits)] if heads == 1 else [])
    for h in range(1, heads):
        near_scores(h)
        return_rows(h - 1, 1)
        far_scores(h)
        return_rows(h - 1, 0)
        soften(h)
        outputs(h)
        send_attn(h)
        grads(h, [text_stage(b) for b in range(bits)] if h == heads - 1 else [])

    finish()
    base = starts[-1]
    text_res = r["text_res"]
    text_res[pl.ds(base, 1)] = acc[pl.ds(base, 1)].astype(BF16)

    def gather(b):
        n = seq_count >> (b + 1)
        at = starts[b + 1]
        return start(
            text_res.at[pl.ds(at, n)], text_res.at[pl.ds(at, n)],
            r["gather_ss"].at[b], r["gather_rs"].at[b], seq_id(partner_at[b]),
        )

    for copy in attn_copies:
        copy.wait_recv()
    gate_acc = r["gate_acc"]
    piece = 384 if my_cols % 384 == 0 else 128
    for c in range(my_cols // piece):
        at = slice(c * piece, (c + 1) * piece)
        total = jnp.zeros((tile, piece), F32)
        for step in range(head_count):
            for h in range(heads):
                left = attn_ref[h] if step == 0 else r["attn_in"][step - 1, h]
                total = total + jnp.dot(
                    left, wall_ref[step, part_of(h), at], preferred_element_type=F32
                )
        gate_acc[:, at] = jnp.sum(grad_ref[:, at].astype(F32) * total, axis=0, keepdims=True)
    for place, b in enumerate(reversed(range(bits))):
        if place == bits - bits // 2:
            return_rows(heads - 1, 1)
            return_rows(heads - 1, 0)
        gathering = gather(b)
        r["gate_out"][b] = gate_acc[...]
        copy = start(
            r["gate_out"].at[b], r["gate_in"].at[b], r["gate_ss"].at[b], r["gate_rs"].at[b],
            seq_id(partner_at[b]),
        )
        gathering.wait_recv()
        copy.wait_recv()
        gate_acc[...] = gate_acc[...] + r["gate_in"][b]
    gate_all = r["gate_all"]
    gate_all[mine] = gate_acc[...]
    all_copies = []
    for step in range(1, head_count):
        all_copies.append(
            start(
                gate_acc, gate_all.at[mine], r["all_ss"].at[step - 1], r["all_rs"].at[step - 1],
                head_id(peers[step - 1]),
            )
        )
    for i in range(per):
        r["dtk"][i * seg : (i + 1) * seg, :] = text_res[i]
        r["dtv"][i * seg : (i + 1) * seg, :] = text_res[per + i]

    for h in range(heads):
        for k in (1, 0):
            total = col_sum(0, h, k)
            for fi, dr in enumerate(far_rows):
                came = row_to[opposite[dr]][1]
                guarded(came, back_rows[fi, h, k].wait_recv)
                got = r["brow_in"][fi, h, k].astype(F32)
                total = total + (got if came is None else jnp.where(came, got, 0.0))
            if k == 0:
                r["dk"][:, part_of(h)] = (
                    total * cos_ref[...] - partner(total) * sin_ref[...]
                ).astype(BF16)
            else:
                r["dv"][:, part_of(h)] = total.astype(BF16)
    for copy in all_copies:
        copy.wait_recv()
    for i in range(head_count):
        r["dgate"][:, i * my_cols : (i + 1) * my_cols] = gate_all[i]
    for copy, ok in sent:
        guarded(ok, copy.wait_send)


def leave_kernel(count, *refs):
    sources, targets, held = refs[:count], refs[count : 2 * count], refs[2 * count : 3 * count]
    in_s, out_s = refs[3 * count :]
    ins = [pltpu.make_async_copy(sources[i], held[i], in_s.at[i]) for i in range(count)]
    outs = [pltpu.make_async_copy(held[i], targets[i], out_s.at[i]) for i in range(count)]
    for copy in ins:
        copy.start()
    for i in range(count):
        ins[i].wait()
        outs[i].start()
    for copy in outs:
        copy.wait()


def on_device(
    query_in,
    key_in,
    value_in,
    text_keys,
    text_values,
    text_mask,
    window_reach,
    tile_map,
    out_weight,
    gate_scale,
    grad_out,
):
    tile, width = query_in.shape
    heads = width // HEAD_DIM
    text = text_keys.shape[0]
    seq_count = lax.axis_size("seq")
    head_count = lax.axis_size("head")
    row_count = seq_count // COLS
    my_cols = grad_out.shape[1]
    row_deltas = (0,) if row_count == 1 else (0, 1) if row_count == 2 else (0, -1, 1)
    nr = len(row_deltas)
    nb = 3 * nr
    nf = max(nr - 1, 1)
    peers = max(head_count - 1, 1)
    bits = seq_count.bit_length() - 1
    seg = 2 * text // seq_count
    dma = pltpu.SemaphoreType.DMA
    vmem = pl.BlockSpec(memory_space=pltpu.VMEM)
    smem = pl.BlockSpec(memory_space=pltpu.SMEM)
    hbm = pl.BlockSpec(memory_space=pl.ANY)
    lanes = lane_tables()
    inputs = [
        ("tile", tile_map, smem),
        ("reach", window_reach, smem),
        ("lanes_hbm", jnp.asarray(lanes), hbm),
        ("q_hbm", query_in, hbm),
        ("k_hbm", key_in, hbm),
        ("v_hbm", value_in, hbm),
        ("tk_hbm", text_keys, hbm),
        ("tv_hbm", text_values, hbm),
        ("mask_hbm", text_mask[None, :], hbm),
        ("w_hbm", out_weight, hbm),
        ("gate_hbm", gate_scale[None, :], hbm),
        ("grad_hbm", grad_out, hbm),
    ]
    outputs = [
        ("dq", (tile, width), BF16),
        ("dk", (tile, width), BF16),
        ("dv", (tile, width), BF16),
        ("dtk", (text, width), BF16),
        ("dtv", (text, width), BF16),
        ("dgate", (1, head_count * my_cols), F32),
    ]
    buffers = [
        ("lanes", lanes.shape, F32),
        ("q", (tile, width), BF16),
        ("k", (tile, width), BF16),
        ("v", (tile, width), BF16),
        ("tk", (text, width), BF16),
        ("tv", (text, width), BF16),
        ("mask", (1, text), jnp.int32),
        ("gate", (1, my_cols), F32),
        ("grad", (tile, my_cols), BF16),
        ("qr", (tile, width), BF16),
        ("kv", (heads, nb, 2, tile, HEAD_DIM), BF16),
        ("part", (heads, nb, 2, tile, HEAD_DIM), BF16),
        ("cos", (tile, HEAD_DIM), F32),
        ("sin", (tile, HEAD_DIM), F32),
        ("wall", (head_count, width, my_cols), BF16),
        ("ga", (tile, width), BF16),
        ("ga32", (tile, width), F32),
        ("proj", (tile, my_cols), BF16),
        ("part_out", (peers, tile, width), BF16),
        ("part_in", (peers, tile, width), BF16),
        ("attn", (heads, tile, HEAD_DIM), BF16),
        ("attn_in", (peers, heads, tile, HEAD_DIM), BF16),
        ("s", (nb * tile + text, tile), F32),
        ("m", (1, tile), F32),
        ("l", (1, tile), F32),
        ("o", (HEAD_DIM, tile), F32),
        ("dqa", (HEAD_DIM, tile), F32),
        ("bcol_in", (2, nr, heads, 2, tile, HEAD_DIM), BF16),
        ("brow_out", (nf, heads, 2, tile, HEAD_DIM), BF16),
        ("brow_in", (nf, heads, 2, tile, HEAD_DIM), BF16),
        ("acc", (seq_count, seg, width), F32),
        ("text_out", (seq_count, seg, width), BF16),
        ("text_in", (seq_count, seg, width), BF16),
        ("text_res", (seq_count, seg, width), BF16),
        ("gate_acc", (1, my_cols), F32),
        ("gate_out", (bits, 1, my_cols), F32),
        ("gate_in", (bits, 1, my_cols), F32),
        ("gate_all", (head_count, 1, my_cols), F32),
    ]
    semaphores = [("load_s", (10,))]
    for name, shape in (
        ("row", (nf, heads, 2)),
        ("col", (2, nr, heads, 2)),
        ("w", (peers,)),
        ("swap", (peers,)),
        ("part", (peers,)),
        ("attn", (peers, heads)),
        ("bcol", (2, nr, heads, 2)),
        ("brow", (nf, heads, 2)),
        ("text", (bits,)),
        ("gather", (bits,)),
        ("gate", (bits,)),
        ("all", (peers,)),
    ):
        semaphores += [(name + "_ss", shape), (name + "_rs", shape)]
    names = [entry[0] for entry in inputs + outputs + buffers + semaphores]
    results = pl.pallas_call(
        functools.partial(mega_kernel, row_deltas, row_count, seq_count, head_count, names),
        out_shape=[jax.ShapeDtypeStruct(shape, kind) for _, shape, kind in outputs],
        in_specs=[spec for _, _, spec in inputs],
        out_specs=[vmem] * len(outputs),
        scratch_shapes=[pltpu.VMEM(shape, kind) for _, shape, kind in buffers]
        + [dma(shape) for _, shape in semaphores],
        compiler_params=pltpu.CompilerParams(
            collective_id=0, has_side_effects=True, vmem_limit_bytes=60 * 1024 * 1024
        ),
    )(*[array for _, array, _ in inputs])
    count = len(outputs)
    results = pl.pallas_call(
        functools.partial(leave_kernel, count),
        out_shape=[jax.ShapeDtypeStruct(shape, kind) for _, shape, kind in outputs],
        in_specs=[hbm] * count,
        out_specs=[hbm] * count,
        scratch_shapes=[pltpu.VMEM(shape, kind) for _, shape, kind in outputs]
        + [dma((count,)), dma((count,))],
    )(*results)
    return (*results[:5], results[5].reshape(-1))


def solution(mesh):
    placed = (
        P("seq", "head"),
        P("seq", "head"),
        P("seq", "head"),
        P(None, "head"),
        P(None, "head"),
        P(),
        P("head", None),
        P(),
        P("head", None),
        P(),
        P("seq", "head"),
    )
    return jax.shard_map(
        on_device,
        mesh=mesh,
        in_specs=placed,
        out_specs=(
            P("seq", "head"),
            P("seq", "head"),
            P("seq", "head"),
            P(None, "head"),
            P(None, "head"),
            P(),
        ),
        check_vma=False,
    )
```
